128 devices in a mesh: patch: 2 (over core), cells: 64 (over y, x, z).
Axes of the slice: x: 4, y: 4, z: 4, core: 2. Of those that a mesh axis runs over, the one named last changes fastest.
Arguments:
- features: bfloat16 [128, 1024, 512], P('cells', 'patch'), may hold values from -6 to 6
- hilbert_rank: int32 [128, 32], P('cells', 'patch'), may hold values from 0 to 4095, as said below
- valid_count: int32 [128, 32], P('cells', 'patch'), may hold values from 1 to 32
- norm_gains: float32 [3, 512], replicated
- w_qkv: bfloat16 [512, 1536], replicated
- w_out: bfloat16 [512, 512], replicated, may hold values from -0.25 to 0.25
- w_up: bfloat16 [2, 512, 2048], replicated, may hold values from -0.25 to 0.25
- w_down: bfloat16 [2, 2048, 512], replicated, may hold values from -0.125 to 0.125
Outputs:
- final: bfloat16 [128, 1024, 512], P('cells', 'patch')
The draws below stay inside these ranges and needn't reach their ends.
Inputs may be any that keep to these rules, and one draw needn't show every extreme that they name: `hilbert_rank`: a permutation of all cells; a cell keeps its half of a patch (its index within the patch divided by 16 stays the same); the 32 cells of one device go to exactly 32 owners along cells (the device itself may be one), 1 cells to each.
All inputs are finite; a program needn't handle non-finite values.
Results may differ from the reference program's by a relative error of at most 0.013.
The reference program's roundings to bfloat16 on the way count: a program that leaves them out, or rounds other values in their place, can miss the bound.
Values may be sent and summed in bfloat16 or wider, within the bound.
A program may use at most 128 MiB of HBM per device.

```python
import jax
import jax.numpy as jnp
from jax import lax

C = 512
HEADS = 32
FF = 2048
PATCH = 1024
CELL = 32
LAYERS = 2
PGROUP = 2
PATCHES = 128
CAP = 1


def draw_hilbert_rank(key, part):
    owners = PATCHES // PGROUP
    half_cells = PATCH // CELL // 2
    cells_dev = PGROUP * half_cells
    local_ids = jnp.arange(cells_dev, dtype=jnp.int32)
    stride_index = local_ids // CAP
    arrival = local_ids
    blocks = []
    for flank in range(2):
        base = jax.random.fold_in(key, 17 + flank)
        first_key, second_key, third_key = jax.random.split(base, 3)
        lineup = jax.random.permutation(first_key, owners).astype(jnp.int32)
        targets = jax.random.permutation(second_key, owners).astype(jnp.int32)
        shuffles = jax.vmap(lambda k: jax.random.permutation(k, cells_dev))(jax.random.split(third_key, owners)).astype(jnp.int32)
        destination = targets[(lineup[:, None] + stride_index[None, :]) % owners]
        placed = shuffles[destination, arrival[None, :]]
        patch_index = destination * PGROUP + placed // half_cells
        inside = flank * half_cells + placed % half_cells
        blocks.append(patch_index * (2 * half_cells) + inside)
    ranking = jnp.stack(blocks, axis=1).reshape(owners, 2, PGROUP, half_cells)
    ranking = jnp.transpose(ranking, (0, 2, 1, 3)).reshape(PATCHES, 2 * half_cells)
    return ranking.astype(jnp.int32)


def draw_norm_gains(key, part):
    first_key = jax.random.fold_in(jax.random.fold_in(key, 5), 0)
    gains = jax.random.uniform(first_key, (LAYERS + 1, C), jnp.float32, 0.5, 1.5)
    return gains.astype(jnp.float32)


def draw_w_qkv(key, part):
    query_key, key_key, value_key = jax.random.split(jax.random.fold_in(key, 9), 3)
    deviation = C ** (-0.5)
    query_part = jax.random.normal(query_key, (C, C), jnp.float32) * deviation
    value_part = jax.random.normal(value_key, (C, C), jnp.float32) * deviation
    key_part = jax.random.normal(key_key, (C, C), jnp.float32) * deviation
    return jnp.concatenate([query_part, key_part, value_part], axis=1).astype(jnp.bfloat16)


def place_ends(values, own_key, smallest, high):
    dims = values.shape
    place = [jax.random.randint(jax.random.fold_in(own_key, axis), (), 0, dims[axis]) for axis in range(len(dims))]
    values = values.at[tuple(place)].set(smallest)
    longest = dims.index(max(dims))
    place[longest] = (place[longest] + 1) % dims[longest]
    return values.at[tuple(place)].set(high)


def block_scale(rng, dims, shards, least, high):
    def one(position, parts):
        steps = jax.random.uniform(jax.random.fold_in(jax.random.fold_in(rng, 6), position), (parts,), jnp.float32, least / len(shards), high / len(shards))
        return jnp.repeat(jnp.exp(steps), dims[position] // parts).reshape((-1,) + (1,) * (len(dims) - position - 1))

    level = one(*shards[0])
    for cut in shards[1:]:
        level = level * one(*cut)
    return level


def gaussian(key, shape, scale, limit, cuts=(), held_as=jnp.bfloat16):
    array = scale * jax.random.normal(key, shape, jnp.float32)
    if cuts:
        array = array * block_scale(key, shape, cuts, -0.22, 0.18)
    return jnp.clip(array, -limit, limit).astype(held_as)


def setup_inputs(seed: int = 0) -> dict:
    arg_keys = jax.random.split(jax.random.key(seed), 9)
    features = gaussian(arg_keys[0], (PATCHES, PATCH, C), 1.0, 6.0, ((0, 64), (1, 2)))
    hilbert_rank = draw_hilbert_rank(jax.random.fold_in(arg_keys[8], 71), 0)
    valid_count = place_ends(jax.random.randint(arg_keys[2], (PATCHES, PATCH // CELL), 1, CELL + 1), jax.random.fold_in(arg_keys[2], 1), 1, CELL).astype(jnp.int32)
    norm_gains = draw_norm_gains(jax.random.fold_in(arg_keys[8], 71), 0)
    w_qkv = draw_w_qkv(jax.random.fold_in(arg_keys[8], 71), 0)
    w_out = gaussian(arg_keys[5], (C, C), C ** -0.5, 0.25)
    w_up = gaussian(arg_keys[6], (LAYERS, C, FF), C ** -0.5, 0.25)
    w_down = gaussian(arg_keys[7], (LAYERS, FF, C), FF ** -0.5, 0.125)
    return dict(features=features, hilbert_rank=hilbert_rank, valid_count=valid_count, norm_gains=norm_gains, w_qkv=w_qkv, w_out=w_out, w_up=w_up, w_down=w_down)


EPSILON = 1e-05

def norm_rows(values, gains):
    center = values - lax.optimization_barrier(jnp.mean(values, axis=-1, keepdims=True))
    spread = lax.optimization_barrier(jnp.mean(center * center, axis=-1, keepdims=True))
    return (center * lax.rsqrt(spread + EPSILON) * gains).astype(jnp.bfloat16)

def split_heads(matrix):
    row_count = matrix.shape[0]
    head_depth = matrix.shape[1] // HEADS
    return jnp.moveaxis(matrix.reshape(row_count, HEADS // 4, 4, head_depth), 1, 0)

def attend(queries, key_rows, value_rows, visible):
    head_depth = queries.shape[1] // HEADS
    scaling = head_depth ** (-0.5)

    def head_group(operands):
        query_block, key_block, value_block = operands
        scores = jnp.einsum('qhd,khd->hqk', query_block.astype(jnp.float32), key_block.astype(jnp.float32)) * scaling
        scores = jnp.where(visible[None, None, :], scores, -jnp.inf)
        highest = lax.optimization_barrier(jnp.max(scores, axis=-1, keepdims=True))
        exponent = jnp.exp(scores - highest)
        totals = lax.optimization_barrier(jnp.sum(exponent, axis=-1))
        weights = exponent.astype(jnp.bfloat16)
        mixture = jnp.einsum('hqk,khd->qhd', weights.astype(jnp.float32), value_block.astype(jnp.float32))
        return mixture / jnp.swapaxes(totals, 0, 1)[:, :, None]
    outputs = lax.map(head_group, (split_heads(queries), split_heads(key_rows), split_heads(value_rows)))
    return jnp.moveaxis(outputs, 0, 1).reshape(queries.shape).astype(jnp.bfloat16)

def attention_part(rows, visible, gain_row, w_qkv, w_out):
    width = rows.shape[1]
    normed = norm_rows(rows.astype(jnp.float32), gain_row)
    projected = jnp.dot(normed, w_qkv, preferred_element_type=jnp.float32).astype(jnp.bfloat16)
    attended = attend(projected[:, :width], projected[:, width:2 * width], projected[:, 2 * width:], visible)
    added = rows.astype(jnp.float32) + jnp.dot(attended, w_out, preferred_element_type=jnp.float32)
    return added.astype(jnp.bfloat16)

def mlp_part(rows, gain_row, w_up_layer, w_down_layer):
    normed = norm_rows(rows.astype(jnp.float32), gain_row)
    raised = jnp.dot(normed, w_up_layer, preferred_element_type=jnp.float32)
    hidden = jax.nn.gelu(raised, approximate=True).astype(jnp.bfloat16)
    added = rows.astype(jnp.float32) + jnp.dot(hidden, w_down_layer, preferred_element_type=jnp.float32)
    return added.astype(jnp.bfloat16)

def reference(features, hilbert_rank, valid_count, norm_gains, w_qkv, w_out, w_up, w_down):
    patches, patch_len, width = features.shape
    per_patch = valid_count.shape[1]
    cell_len = patch_len // per_patch
    positions = jnp.arange(cell_len, dtype=jnp.int32)
    visible = (positions[None, None, :] < valid_count[:, :, None]).reshape(patches, patch_len)

    def first_patch(rows):
        return mlp_part(rows, norm_gains[0], w_up[0], w_down[0])
    first = lax.map(first_patch, features)
    ranks = hilbert_rank.reshape(-1).astype(jnp.int32)
    cells_home = first.reshape(patches * per_patch, cell_len, width)
    curve = jnp.zeros_like(cells_home).at[ranks].set(cells_home).reshape(patches, patch_len, width)
    curve_count = jnp.zeros_like(ranks).at[ranks].set(valid_count.reshape(-1)).reshape(patches, per_patch)
    curve_visible = (positions[None, None, :] < curve_count[:, :, None]).reshape(patches, patch_len)

    def second_patch(operands):
        rows, mask_row = operands
        middle = attention_part(rows, mask_row, norm_gains[1], w_qkv, w_out)
        return mlp_part(middle, norm_gains[2], w_up[1], w_down[1])
    second = lax.map(second_patch, (curve, curve_visible))
    returned = second.reshape(patches * per_patch, cell_len, width)[ranks].reshape(patches, patch_len, width)
    return jnp.where(visible[:, :, None], returned, jnp.zeros((), jnp.bfloat16))
```

```python
import functools
import itertools
import random

import jax
import jax.numpy as jnp
from jax import lax
from jax.experimental import pallas as pl
from jax.experimental.pallas import tpu as pltpu
from jax.sharding import PartitionSpec as P

MESH = pl.DeviceIdType.MESH
EPSILON = 1e-05
C = 512
FF = 2048
CELL = 32
SIDE = 4
SLOTS = SIDE**3
CELLS_DEV = 32
HALF_CELLS = 16
HALF_ROWS = 512
PATCH_ROWS = 1024
GROUPS = 4
GROUP_LANES = 128
GROUP_HEADS = 8
DEPTH = 16
TM = 128
TQ = 64
TK = 128
VMEM_LIMIT = 60 * 1024 * 1024

OFFSETS = [o for o in itertools.product(range(SIDE), repeat=3) if o != (0, 0, 0)]
random.Random(0).shuffle(OFFSETS)


def slot_number(offset):
    return (offset[0] * SIDE + offset[1]) * SIDE + offset[2]


def coordinates():
    me = lax.axis_index("cells")
    return me // (SIDE * SIDE), (me // SIDE) % SIDE, me % SIDE


def peer(offset, sign):
    y, x, z = coordinates()
    ys = (y + sign * offset[0] + SIDE) % SIDE
    xs = (x + sign * offset[1] + SIDE) % SIDE
    zs = (z + sign * offset[2] + SIDE) % SIDE
    return (ys * SIDE + xs) * SIDE + zs


def norm_rows(values, gains):
    center = values - jnp.mean(values, axis=-1, keepdims=True)
    spread = jnp.mean(center * center, axis=-1, keepdims=True)
    return (center * lax.rsqrt(spread + EPSILON) * gains).astype(jnp.bfloat16)


def mlp_rows(rows, gain_row, w_up, w_down):
    normed = norm_rows(rows, gain_row)
    raised = jnp.dot(normed, w_up, preferred_element_type=jnp.float32)
    hidden = jax.nn.gelu(raised, approximate=True).astype(jnp.bfloat16)
    return rows + jnp.dot(hidden, w_down, preferred_element_type=jnp.float32)


def put_rows(ref, start, rows):
    base = pl.multiple_of(start // 8 * 8, 8)
    shift = start - base
    padded = jnp.concatenate([rows, jnp.zeros((8, C), jnp.float32)], axis=0)
    moved = pltpu.roll(padded, shift, 0)
    position = lax.broadcasted_iota(jnp.int32, (8, C), 0)
    ref[pl.ds(base, 8), :] = jnp.where(position < shift, ref[pl.ds(base, 8), :], moved[:8])
    ref[pl.ds(pl.multiple_of(base + 8, 8), CELL), :] = moved[8:]


def take_rows(ref, start):
    base = pl.multiple_of(start // 8 * 8, 8)
    window = ref[pl.ds(base, CELL + 8), :]
    ahead = start - base
    return pltpu.roll(window, jnp.where(ahead == 0, 0, CELL + 8 - ahead), 0)[:CELL]


def first_kernel(
    rank_ref, count_ref, features, gains, up_hbm, down_hbm,
    send, labels, slots, packed, w_up, w_down, offsets, slot_labels, sems,
):
    copies = [
        pltpu.make_async_copy(up_hbm.at[0], w_up, sems.at[0]),
        pltpu.make_async_copy(down_hbm.at[0], w_down, sems.at[1]),
    ]
    for copy in copies:
        copy.start()
    y, x, z = coordinates()

    def clear(slot, carry):
        slot_labels[slot] = 0
        return carry

    lax.fori_loop(0, SLOTS, clear, 0)

    def pack(cell, start):
        rank = rank_ref[cell // HALF_CELLS, cell % HALF_CELLS]
        count = count_ref[cell // HALF_CELLS, cell % HALF_CELLS]
        owner = rank // (2 * CELLS_DEV)
        patch = (rank // CELLS_DEV) % 2
        oy = (owner // (SIDE * SIDE) - y + SIDE) % SIDE
        ox = ((owner // SIDE) % SIDE - x + SIDE) % SIDE
        oz = (owner % SIDE - z + SIDE) % SIDE
        slot = (oy * SIDE + ox) * SIDE + oz
        slots[cell] = slot
        slot_labels[slot] = count + 64 * patch
        offsets[cell] = start
        cell_row = pl.multiple_of(cell * CELL, CELL)
        put_rows(packed, start, features[pl.ds(cell_row, CELL), :].astype(jnp.float32))
        return start + count

    total = lax.fori_loop(0, CELLS_DEV, pack, 0)

    def label(slot, carry):
        labels[slot] = jnp.full((1, 128), slot_labels[slot], jnp.int32)
        return carry

    lax.fori_loop(0, SLOTS, label, 0)
    for copy in copies:
        copy.wait()

    def tile(step, carry):
        rows = pl.ds(pl.multiple_of(step * TM, TM), TM)
        packed[rows, :] = mlp_rows(packed[rows, :], gains[0:1, :], w_up[...], w_down[...])
        return carry

    lax.fori_loop(0, (total + TM - 1) // TM, tile, 0)

    def unpack(cell, carry):
        send[slots[cell]] = take_rows(packed, offsets[cell]).astype(jnp.bfloat16)
        return carry

    lax.fori_loop(0, CELLS_DEV, unpack, 0)


def meet():
    core = lax.axis_index("patch")
    barrier = pltpu.get_barrier_semaphore()
    for offset in OFFSETS:
        pl.semaphore_signal(barrier, inc=1, device_id=(core, peer(offset, 1)), device_id_type=MESH)
    pl.semaphore_signal(
        barrier, inc=1, device_id=(1 - core, lax.axis_index("cells")), device_id_type=MESH
    )
    pl.semaphore_wait(barrier, SLOTS)


def forward_kernel(
    send, labels, own, other, own_labels, other_labels,
    arrived, arrived_labels, send_sem, recv_sem, label_send, label_recv,
    keep_sem, pass_sem, got_sem, tail_sem,
):
    core = lax.axis_index("patch")
    here = lax.axis_index("cells")
    sibling = (1 - core, here)
    meet()
    local = pltpu.make_async_copy(send.at[0], arrived.at[0], recv_sem.at[0])
    local_labels = pltpu.make_async_copy(labels.at[0], arrived_labels.at[0], label_recv.at[0])
    local.start()
    local_labels.start()
    copies = [local]
    label_copies = [local_labels]
    for offset in OFFSETS:
        slot = slot_number(offset)
        to = (core, peer(offset, 1))
        label_copy = pltpu.make_async_remote_copy(
            labels.at[slot], arrived_labels.at[slot], label_send.at[slot], label_recv.at[slot],
            device_id=to, device_id_type=MESH,
        )
        copy = pltpu.make_async_remote_copy(
            send.at[slot], arrived.at[slot], send_sem.at[slot], recv_sem.at[slot],
            device_id=to, device_id_type=MESH,
        )
        label_copy.start()
        copy.start()
        label_copies.append(label_copy)
        copies.append(copy)
    keeps = []
    passes = []
    for index, copy in enumerate(copies):
        slot = 0 if index == 0 else slot_number(OFFSETS[index - 1])
        if index == 0:
            copy.wait()
        else:
            copy.wait_recv()
        keep = pltpu.make_async_copy(arrived.at[slot], own.at[slot], keep_sem.at[slot])
        onward = pltpu.make_async_remote_copy(
            arrived.at[slot], other.at[slot], pass_sem.at[slot], got_sem.at[slot],
            device_id=sibling, device_id_type=MESH,
        )
        keep.start()
        onward.start()
        keeps.append(keep)
        passes.append(onward)
    for index, copy in enumerate(label_copies):
        if index == 0:
            copy.wait()
        else:
            copy.wait_recv()
    keep_labels = pltpu.make_async_copy(arrived_labels, own_labels, tail_sem.at[0])
    pass_labels = pltpu.make_async_remote_copy(
        arrived_labels, other_labels, tail_sem.at[1], tail_sem.at[2],
        device_id=sibling, device_id_type=MESH,
    )
    keep_labels.start()
    pass_labels.start()
    for copy in copies[1:]:
        copy.wait_send()
    for copy in label_copies[1:]:
        copy.wait_send()
    for keep in keeps:
        keep.wait()
    for onward in passes:
        onward.wait()
    keep_labels.wait()
    pass_labels.wait()


def layer_kernel(
    own_labels, other_labels, own, other, gains, qkv_hbm, out_hbm, up_hbm, down_hbm,
    send, packed, queries, keys, values, mixed, w_qkv, w_out, w_up, w_down, offsets, sems,
):
    copies = [
        pltpu.make_async_copy(qkv_hbm, w_qkv, sems.at[0]),
        pltpu.make_async_copy(out_hbm, w_out, sems.at[1]),
        pltpu.make_async_copy(up_hbm.at[1], w_up, sems.at[2]),
        pltpu.make_async_copy(down_hbm.at[1], w_down, sems.at[3]),
    ]
    for copy in copies:
        copy.start()

    def pack_own(slot, starts):
        label = own_labels[slot, 0]
        patch = label // 64
        count = label % 64
        start = jnp.where(patch == 0, starts[0], starts[1])

        @pl.when(count > 0)
        def _():
            offsets[slot] = start
            put_rows(packed.at[patch], start, own[slot].astype(jnp.float32))

        first = jnp.where(patch == 0, count, 0)
        return starts[0] + first, starts[1] + count - first

    query_rows = lax.fori_loop(0, SLOTS, pack_own, (jnp.int32(0), jnp.int32(0)))

    def pack_other(slot, starts):
        label = other_labels[slot, 0]
        patch = label // 64
        count = label % 64
        start = jnp.where(patch == 0, starts[0], starts[1])

        @pl.when(count > 0)
        def _():
            put_rows(packed.at[patch], start, other[slot].astype(jnp.float32))

        first = jnp.where(patch == 0, count, 0)
        return starts[0] + first, starts[1] + count - first

    key_rows = lax.fori_loop(0, SLOTS, pack_other, query_rows)
    for copy in copies:
        copy.wait()
    lane = lax.broadcasted_iota(jnp.int32, (1, GROUP_LANES), 1) // DEPTH
    head_masks = [(lane == head).astype(jnp.float32) for head in range(GROUP_HEADS)]

    def project(patch, key_count, step, carry):
        base = pl.multiple_of(step * TM, TM)
        rows = pl.ds(base, TM)
        normed = norm_rows(packed[patch, rows, :], gains[1:2, :])
        projected = jnp.dot(normed, w_qkv[...], preferred_element_type=jnp.float32)
        projected = projected.astype(jnp.bfloat16)
        seen = lax.broadcasted_iota(jnp.int32, (TM, GROUP_LANES), 0) + base < key_count
        for group in range(GROUPS):
            low = group * GROUP_LANES
            queries[group, rows, :] = projected[:, low : low + GROUP_LANES] * 0.25
            keys[group, rows, :] = projected[:, C + low : C + low + GROUP_LANES]
            value = projected[:, 2 * C + low : 2 * C + low + GROUP_LANES].astype(jnp.float32)
            values[group, rows, :GROUP_LANES] = jnp.where(seen, value, 0.0).astype(jnp.bfloat16)
            values[group, rows, GROUP_LANES:] = jnp.where(seen, 1.0, 0.0).astype(jnp.bfloat16)
        return carry

    def attend(key_span, step, carry):
        group = step % GROUPS
        rows = pl.ds(pl.multiple_of((step // GROUPS) * TQ, TQ), TQ)
        query = queries[group, rows, :].astype(jnp.float32)
        stacked = jnp.concatenate([query * mask for mask in head_masks], axis=0)
        scores = lax.dot_general(
            stacked.astype(jnp.bfloat16), keys[group, :key_span, :],
            (((1,), (1,)), ((), ())), preferred_element_type=jnp.float32,
        )
        highest = jnp.max(scores, axis=1, keepdims=True)
        weights = jnp.exp(scores - highest).astype(jnp.bfloat16)
        mixture = jnp.dot(weights, values[group, :key_span, :], preferred_element_type=jnp.float32)
        top = jnp.zeros((TQ, GROUP_LANES), jnp.float32)
        total = jnp.zeros((TQ, GROUP_LANES), jnp.float32)
        for head in range(GROUP_HEADS):
            part = mixture[head * TQ : (head + 1) * TQ, :]
            chosen = lane == head
            top = jnp.where(chosen, part[:, :GROUP_LANES], top)
            total = jnp.where(chosen, part[:, GROUP_LANES:], total)
        mixed[group, rows, :] = (top / total).astype(jnp.bfloat16)
        return carry

    def finish(patch, step, carry):
        rows = pl.ds(pl.multiple_of(step * TM, TM), TM)
        middle = packed[patch, rows, :]
        for group in range(GROUPS):
            low = group * GROUP_LANES
            middle = middle + jnp.dot(
                mixed[group, rows, :], w_out[low : low + GROUP_LANES, :],
                preferred_element_type=jnp.float32,
            )
        middle = middle.astype(jnp.bfloat16).astype(jnp.float32)
        packed[patch, rows, :] = mlp_rows(middle, gains[2:3, :], w_up[...], w_down[...])
        return carry

    def one_patch(patch, carry):
        query_count = jnp.where(patch == 0, query_rows[0], query_rows[1])
        key_count = jnp.where(patch == 0, key_rows[0], key_rows[1])
        base = pl.multiple_of(key_count // 8 * 8, 8)
        spare = jnp.broadcast_to(packed[patch, 0:1, :], (8, C))
        edge = packed[patch, pl.ds(base, 8), :]
        position = lax.broadcasted_iota(jnp.int32, (8, C), 0)
        packed[patch, pl.ds(base, 8), :] = jnp.where(position < key_count - base, edge, spare)
        packed[patch, pl.ds(pl.multiple_of(base + 8, 8), TK), :] = jnp.broadcast_to(spare[:1], (TK, C))
        key_tiles = (key_count + TK - 1) // TK
        lax.fori_loop(0, key_tiles, functools.partial(project, patch, key_count), 0)
        steps = (query_count + TQ - 1) // TQ * GROUPS
        for tiles in range(1, PATCH_ROWS // TK + 1):

            @pl.when(key_tiles == tiles)
            def _():
                lax.fori_loop(0, steps, functools.partial(attend, tiles * TK), 0)

        lax.fori_loop(0, (query_count + TM - 1) // TM, functools.partial(finish, patch), 0)
        return carry

    lax.fori_loop(0, 2, one_patch, 0)

    def unpack(slot, carry):
        label = own_labels[slot, 0]

        @pl.when(label > 0)
        def _():
            rows = take_rows(packed.at[label // 64], offsets[slot])
            send[slot] = rows.astype(jnp.bfloat16)

        return carry

    lax.fori_loop(0, SLOTS, unpack, 0)


def return_kernel(slots, counts, send, out, arrived, send_sem, recv_sem):
    core = lax.axis_index("patch")
    meet()
    local = pltpu.make_async_copy(send.at[0], arrived.at[0], recv_sem.at[0])
    local.start()
    copies = []
    for offset in OFFSETS:
        slot = slot_number(offset)
        copy = pltpu.make_async_remote_copy(
            send.at[slot], arrived.at[slot], send_sem.at[slot], recv_sem.at[slot],
            device_id=(core, peer(offset, -1)), device_id_type=MESH,
        )
        copy.start()
        copies.append(copy)
    local.wait()
    for copy in copies:
        copy.wait()
    position = lax.broadcasted_iota(jnp.int32, (CELL, C), 0)
    for cell in range(CELLS_DEV):
        rows = arrived[slots[cell]].astype(jnp.float32)
        count = counts[cell // HALF_CELLS, cell % HALF_CELLS]
        out[cell] = jnp.where(position < count, rows, 0.0).astype(jnp.bfloat16)


def any_spec():
    return pl.BlockSpec(memory_space=pl.ANY)


def vmem_spec():
    return pl.BlockSpec(memory_space=pltpu.VMEM)


def smem_spec():
    return pl.BlockSpec(memory_space=pltpu.SMEM)


def shards(features, hilbert_rank, valid_count, norm_gains, w_qkv, w_out, w_up, w_down):
    slab = jax.ShapeDtypeStruct((SLOTS, CELL, C), jnp.bfloat16)
    label_shape = jax.ShapeDtypeStruct((SLOTS, 1, 128), jnp.int32)
    dma = pltpu.SemaphoreType.DMA
    send, labels, slots = pl.pallas_call(
        first_kernel,
        out_shape=(slab, label_shape, jax.ShapeDtypeStruct((CELLS_DEV,), jnp.int32)),
        in_specs=[smem_spec(), smem_spec(), vmem_spec(), vmem_spec(), any_spec(), any_spec()],
        out_specs=(vmem_spec(), vmem_spec(), smem_spec()),
        scratch_shapes=[
            pltpu.VMEM((CELLS_DEV * CELL + TM, C), jnp.float32),
            pltpu.VMEM((C, FF), jnp.bfloat16),
            pltpu.VMEM((FF, C), jnp.bfloat16),
            pltpu.SMEM((CELLS_DEV,), jnp.int32),
            pltpu.SMEM((SLOTS,), jnp.int32),
            dma((2,)),
        ],
        compiler_params=pltpu.CompilerParams(vmem_limit_bytes=VMEM_LIMIT),
        name="first",
    )(hilbert_rank, valid_count, features.reshape(CELLS_DEV * CELL, C), norm_gains, w_up, w_down)

    own, other, own_labels, other_labels = pl.pallas_call(
        forward_kernel,
        out_shape=(slab, slab, label_shape, label_shape),
        in_specs=[any_spec(), vmem_spec()],
        out_specs=(any_spec(), any_spec(), any_spec(), any_spec()),
        scratch_shapes=[
            pltpu.VMEM((SLOTS, CELL, C), jnp.bfloat16),
            pltpu.VMEM((SLOTS, 1, 128), jnp.int32),
            dma((SLOTS,)), dma((SLOTS,)), dma((SLOTS,)), dma((SLOTS,)),
            dma((SLOTS,)), dma((SLOTS,)), dma((SLOTS,)), dma((3,)),
        ],
        compiler_params=pltpu.CompilerParams(
            collective_id=0, has_side_effects=True, vmem_limit_bytes=VMEM_LIMIT
        ),
        name="forward",
    )(send, labels)

    send = pl.pallas_call(
        layer_kernel,
        out_shape=slab,
        in_specs=[smem_spec(), smem_spec(), vmem_spec(), vmem_spec(), vmem_spec()]
        + [any_spec()] * 4,
        out_specs=vmem_spec(),
        scratch_shapes=[
            pltpu.VMEM((2, PATCH_ROWS + 2 * TK, C), jnp.float32),
            pltpu.VMEM((GROUPS, PATCH_ROWS, GROUP_LANES), jnp.bfloat16),
            pltpu.VMEM((GROUPS, PATCH_ROWS, GROUP_LANES), jnp.bfloat16),
            pltpu.VMEM((GROUPS, PATCH_ROWS, 2 * GROUP_LANES), jnp.bfloat16),
            pltpu.VMEM((GROUPS, HALF_ROWS, GROUP_LANES), jnp.bfloat16),
            pltpu.VMEM((C, 3 * C), jnp.bfloat16),
            pltpu.VMEM((C, C), jnp.bfloat16),
            pltpu.VMEM((C, FF), jnp.bfloat16),
            pltpu.VMEM((FF, C), jnp.bfloat16),
            pltpu.SMEM((SLOTS,), jnp.int32),
            dma((4,)),
        ],
        compiler_params=pltpu.CompilerParams(vmem_limit_bytes=VMEM_LIMIT),
        name="layer",
    )(
        own_labels.reshape(SLOTS, 128), other_labels.reshape(SLOTS, 128), own, other, norm_gains,
        w_qkv, w_out, w_up, w_down,
    )

    out = pl.pallas_call(
        return_kernel,
        out_shape=jax.ShapeDtypeStruct((CELLS_DEV, CELL, C), jnp.bfloat16),
        in_specs=[smem_spec(), smem_spec(), any_spec()],
        out_specs=vmem_spec(),
        scratch_shapes=[
            pltpu.VMEM((SLOTS, CELL, C), jnp.bfloat16),
            dma((SLOTS,)), dma((SLOTS,)),
        ],
        compiler_params=pltpu.CompilerParams(
            collective_id=1, has_side_effects=True, vmem_limit_bytes=VMEM_LIMIT
        ),
        name="homeward",
    )(slots, valid_count, send)
    return out.reshape(features.shape)


def solution(mesh):
    in_specs = (
        P("cells", "patch", None),
        P("cells", "patch"),
        P("cells", "patch"),
        P(),
        P(),
        P(),
        P(),
        P(),
    )
    out_specs = P("cells", "patch", None)
    return jax.shard_map(shards, mesh=mesh, in_specs=in_specs, out_specs=out_specs, check_vma=False)
```

```python
import functools
import itertools
import random

import jax
import jax.numpy as jnp
from jax import lax
from jax.experimental import pallas as pl
from jax.experimental.pallas import tpu as pltpu
from jax.sharding import PartitionSpec as P

MESH = pl.DeviceIdType.MESH
EPSILON = 1e-05
C = 512
FF = 2048
CELL = 32
SIDE = 4
SLOTS = SIDE**3
CELLS_DEV = 32
HALF_CELLS = 16
HALF_ROWS = 512
PATCH_ROWS = 1024
GROUPS = 4
GROUP_LANES = 128
GROUP_HEADS = 8
DEPTH = 16
TM = 128
TQ = 32
TK = 128
STACK = GROUP_HEADS * TQ
VMEM_LIMIT = 60 * 1024 * 1024

OFFSETS = [o for o in itertools.product(range(SIDE), repeat=3) if o != (0, 0, 0)]
random.Random(0).shuffle(OFFSETS)


def slot_number(offset):
    return (offset[0] * SIDE + offset[1]) * SIDE + offset[2]


def coordinates():
    me = lax.axis_index("cells")
    return me // (SIDE * SIDE), (me // SIDE) % SIDE, me % SIDE


def peer(offset, sign):
    y, x, z = coordinates()
    ys = (y + sign * offset[0] + SIDE) % SIDE
    xs = (x + sign * offset[1] + SIDE) % SIDE
    zs = (z + sign * offset[2] + SIDE) % SIDE
    return (ys * SIDE + xs) * SIDE + zs


def norm_rows(values, gains):
    center = values - jnp.mean(values, axis=-1, keepdims=True)
    spread = jnp.mean(center * center, axis=-1, keepdims=True)
    return (center * lax.rsqrt(spread + EPSILON) * gains).astype(jnp.bfloat16)


def mlp_rows(rows, gain_row, w_up, w_down):
    normed = norm_rows(rows, gain_row)
    raised = jnp.dot(normed, w_up, preferred_element_type=jnp.float32)
    hidden = jax.nn.gelu(raised, approximate=True).astype(jnp.bfloat16)
    return rows + jnp.dot(hidden, w_down, preferred_element_type=jnp.float32)


def put_rows(ref, start, rows):
    base = pl.multiple_of(start // 8 * 8, 8)
    shift = start - base
    padded = jnp.concatenate([rows, jnp.zeros((8, C), jnp.float32)], axis=0)
    moved = pltpu.roll(padded, shift, 0)
    position = lax.broadcasted_iota(jnp.int32, (8, C), 0)
    ref[pl.ds(base, 8), :] = jnp.where(position < shift, ref[pl.ds(base, 8), :], moved[:8])
    ref[pl.ds(pl.multiple_of(base + 8, 8), CELL), :] = moved[8:]


def take_rows(ref, start):
    base = pl.multiple_of(start // 8 * 8, 8)
    window = ref[pl.ds(base, CELL + 8), :]
    ahead = start - base
    return pltpu.roll(window, jnp.where(ahead == 0, 0, CELL + 8 - ahead), 0)[:CELL]


def first_kernel(
    rank_ref, count_ref, features, gains, up_hbm, down_hbm,
    send, labels, slots, packed, w_up, w_down, offsets, slot_labels, sems,
):
    copies = [
        pltpu.make_async_copy(up_hbm.at[0], w_up, sems.at[0]),
        pltpu.make_async_copy(down_hbm.at[0], w_down, sems.at[1]),
    ]
    for copy in copies:
        copy.start()
    y, x, z = coordinates()

    def clear(slot, carry):
        slot_labels[slot] = 0
        return carry

    lax.fori_loop(0, SLOTS, clear, 0)

    def pack(cell, start):
        rank = rank_ref[cell // HALF_CELLS, cell % HALF_CELLS]
        count = count_ref[cell // HALF_CELLS, cell % HALF_CELLS]
        owner = rank // (2 * CELLS_DEV)
        patch = (rank // CELLS_DEV) % 2
        oy = (owner // (SIDE * SIDE) - y + SIDE) % SIDE
        ox = ((owner // SIDE) % SIDE - x + SIDE) % SIDE
        oz = (owner % SIDE - z + SIDE) % SIDE
        slot = (oy * SIDE + ox) * SIDE + oz
        slots[cell] = slot
        slot_labels[slot] = count + 64 * patch
        offsets[cell] = start
        cell_row = pl.multiple_of(cell * CELL, CELL)
        put_rows(packed, start, features[pl.ds(cell_row, CELL), :].astype(jnp.float32))
        return start + count

    total = lax.fori_loop(0, CELLS_DEV, pack, 0)

    def label(slot, carry):
        labels[slot] = jnp.full((1, 128), slot_labels[slot], jnp.int32)
        return carry

    lax.fori_loop(0, SLOTS, label, 0)
    for copy in copies:
        copy.wait()

    def tile(step, carry):
        rows = pl.ds(pl.multiple_of(step * TM, TM), TM)
        packed[rows, :] = mlp_rows(packed[rows, :], gains[0:1, :], w_up[...], w_down[...])
        return carry

    lax.fori_loop(0, (total + TM - 1) // TM, tile, 0)

    def unpack(cell, carry):
        send[slots[cell]] = take_rows(packed, offsets[cell]).astype(jnp.bfloat16)
        return carry

    lax.fori_loop(0, CELLS_DEV, unpack, 0)


def meet():
    core = lax.axis_index("patch")
    barrier = pltpu.get_barrier_semaphore()
    for offset in OFFSETS:
        pl.semaphore_signal(barrier, inc=1, device_id=(core, peer(offset, 1)), device_id_type=MESH)
    pl.semaphore_signal(
        barrier, inc=1, device_id=(1 - core, lax.axis_index("cells")), device_id_type=MESH
    )
    pl.semaphore_wait(barrier, SLOTS)


def forward_kernel(
    send, labels, own, other, own_labels, other_labels,
    arrived, arrived_labels, send_sem, recv_sem, label_send, label_recv,
    keep_sem, pass_sem, got_sem, tail_sem,
):
    core = lax.axis_index("patch")
    here = lax.axis_index("cells")
    sibling = (1 - core, here)
    meet()
    local = pltpu.make_async_copy(send.at[0], arrived.at[0], recv_sem.at[0])
    local_labels = pltpu.make_async_copy(labels.at[0], arrived_labels.at[0], label_recv.at[0])
    local.start()
    local_labels.start()
    copies = [local]
    label_copies = [local_labels]
    for offset in OFFSETS:
        slot = slot_number(offset)
        to = (core, peer(offset, 1))
        label_copy = pltpu.make_async_remote_copy(
            labels.at[slot], arrived_labels.at[slot], label_send.at[slot], label_recv.at[slot],
            device_id=to, device_id_type=MESH,
        )
        copy = pltpu.make_async_remote_copy(
            send.at[slot], arrived.at[slot], send_sem.at[slot], recv_sem.at[slot],
            device_id=to, device_id_type=MESH,
        )
        label_copy.start()
        copy.start()
        label_copies.append(label_copy)
        copies.append(copy)
    keeps = []
    passes = []
    for index, copy in enumerate(copies):
        slot = 0 if index == 0 else slot_number(OFFSETS[index - 1])
        if index == 0:
            copy.wait()
        else:
            copy.wait_recv()
        keep = pltpu.make_async_copy(arrived.at[slot], own.at[slot], keep_sem.at[slot])
        onward = pltpu.make_async_remote_copy(
            arrived.at[slot], other.at[slot], pass_sem.at[slot], got_sem.at[slot],
            device_id=sibling, device_id_type=MESH,
        )
        keep.start()
        onward.start()
        keeps.append(keep)
        passes.append(onward)
    for index, copy in enumerate(label_copies):
        if index == 0:
            copy.wait()
        else:
            copy.wait_recv()
    keep_labels = pltpu.make_async_copy(arrived_labels, own_labels, tail_sem.at[0])
    pass_labels = pltpu.make_async_remote_copy(
        arrived_labels, other_labels, tail_sem.at[1], tail_sem.at[2],
        device_id=sibling, device_id_type=MESH,
    )
    keep_labels.start()
    pass_labels.start()
    for copy in copies[1:]:
        copy.wait_send()
    for copy in label_copies[1:]:
        copy.wait_send()
    for keep in keeps:
        keep.wait()
    for onward in passes:
        onward.wait()
    keep_labels.wait()
    pass_labels.wait()


def layer_kernel(
    own_labels, other_labels, own, other, gains, qkv_hbm, out_hbm, up_hbm, down_hbm,
    send, packed, queries, keys, values, mixed, w_qkv, w_out, w_up, w_down, offsets, sems,
):
    copies = [
        pltpu.make_async_copy(qkv_hbm, w_qkv, sems.at[0]),
        pltpu.make_async_copy(out_hbm, w_out, sems.at[1]),
        pltpu.make_async_copy(up_hbm.at[1], w_up, sems.at[2]),
        pltpu.make_async_copy(down_hbm.at[1], w_down, sems.at[3]),
    ]
    for copy in copies:
        copy.start()

    def pack_own(slot, starts):
        label = own_labels[slot, 0]
        patch = label // 64
        count = label % 64
        start = jnp.where(patch == 0, starts[0], starts[1])

        @pl.when(count > 0)
        def _():
            offsets[slot] = start
            put_rows(packed.at[patch], start, own[slot].astype(jnp.float32))

        first = jnp.where(patch == 0, count, 0)
        return starts[0] + first, starts[1] + count - first

    query_rows = lax.fori_loop(0, SLOTS, pack_own, (jnp.int32(0), jnp.int32(0)))

    def pack_other(slot, starts):
        label = other_labels[slot, 0]
        patch = label // 64
        count = label % 64
        start = jnp.where(patch == 0, starts[0], starts[1])

        @pl.when(count > 0)
        def _():
            put_rows(packed.at[patch], start, other[slot].astype(jnp.float32))

        first = jnp.where(patch == 0, count, 0)
        return starts[0] + first, starts[1] + count - first

    key_rows = lax.fori_loop(0, SLOTS, pack_other, query_rows)
    for copy in copies:
        copy.wait()
    lane = lax.broadcasted_iota(jnp.int32, (1, GROUP_LANES), 1) // DEPTH
    head_masks = [(lane == head).astype(jnp.float32) for head in range(GROUP_HEADS)]

    def project(patch, key_count, step, carry):
        base = pl.multiple_of(step * TM, TM)
        rows = pl.ds(base, TM)
        normed = norm_rows(packed[patch, rows, :], gains[1:2, :])
        projected = jnp.dot(normed, w_qkv[...], preferred_element_type=jnp.float32)
        projected = projected.astype(jnp.bfloat16)
        seen = lax.broadcasted_iota(jnp.int32, (GROUP_LANES, TM), 1) + base < key_count
        ones = lax.broadcasted_iota(jnp.int32, (DEPTH, TM), 1) + base < key_count
        for group in range(GROUPS):
            low = group * GROUP_LANES
            queries[group, rows, :] = projected[:, low : low + GROUP_LANES] * 0.25
            keys[group, rows, :] = projected[:, C + low : C + low + GROUP_LANES]
            value = projected[:, 2 * C + low : 2 * C + low + GROUP_LANES].astype(jnp.float32)
            values[group, :GROUP_LANES, rows] = jnp.where(seen, value.T, 0.0).astype(jnp.bfloat16)
            values[group, GROUP_LANES:, rows] = jnp.where(ones, 1.0, 0.0).astype(jnp.bfloat16)
        return carry

    fold = lax.broadcasted_iota(jnp.int32, (TQ, STACK), 1) % TQ
    fold = fold == lax.broadcasted_iota(jnp.int32, (TQ, STACK), 0)
    fold = fold.astype(jnp.float32).astype(jnp.bfloat16)
    block = lax.broadcasted_iota(jnp.int32, (GROUP_LANES, STACK), 0) // DEPTH
    block = block == lax.broadcasted_iota(jnp.int32, (GROUP_LANES, STACK), 1) // TQ

    def attend(key_span, step, carry):
        rows = pl.ds(pl.multiple_of(step * TQ, TQ), TQ)

        def score(group):
            query = queries[group, rows, :].astype(jnp.float32)
            stacked = jnp.concatenate([query * mask for mask in head_masks], axis=0)
            return lax.dot_general(
                keys[group, :key_span, :], stacked.astype(jnp.bfloat16),
                (((1,), (1,)), ((), ())), preferred_element_type=jnp.float32,
            )

        def weigh(scores):
            highest = jnp.max(scores, axis=0, keepdims=True)
            return jnp.exp(scores - highest).astype(jnp.bfloat16)

        def mix(group, weights):
            mixture = jnp.dot(
                values[group, :, :key_span], weights, preferred_element_type=jnp.float32
            )
            top = mixture[:GROUP_LANES] / mixture[GROUP_LANES : GROUP_LANES + 1]
            return jnp.where(block, top, 0.0).astype(jnp.bfloat16)

        def store(group, top):
            low = group * GROUP_LANES
            mixed[rows, low : low + GROUP_LANES] = lax.dot_general(
                fold, top, (((1,), (1,)), ((), ())), preferred_element_type=jnp.float32
            ).astype(jnp.bfloat16)

        scores = [score(group) for group in range(GROUPS)]
        weights = [weigh(value) for value in scores]
        tops = [mix(group, value) for group, value in enumerate(weights)]
        for group, top in enumerate(tops):
            store(group, top)
        return carry

    def finish(patch, step, carry):
        rows = pl.ds(pl.multiple_of(step * TM, TM), TM)
        middle = packed[patch, rows, :] + jnp.dot(
            mixed[rows, :], w_out[...], preferred_element_type=jnp.float32
        )
        middle = middle.astype(jnp.bfloat16).astype(jnp.float32)
        packed[patch, rows, :] = mlp_rows(middle, gains[2:3, :], w_up[...], w_down[...])
        return carry

    def one_patch(patch, carry):
        query_count = jnp.where(patch == 0, query_rows[0], query_rows[1])
        key_count = jnp.where(patch == 0, key_rows[0], key_rows[1])
        base = pl.multiple_of(key_count // 8 * 8, 8)
        spare = jnp.broadcast_to(packed[patch, 0:1, :], (8, C))
        edge = packed[patch, pl.ds(base, 8), :]
        position = lax.broadcasted_iota(jnp.int32, (8, C), 0)
        packed[patch, pl.ds(base, 8), :] = jnp.where(position < key_count - base, edge, spare)
        packed[patch, pl.ds(pl.multiple_of(base + 8, 8), TK), :] = jnp.broadcast_to(spare[:1], (TK, C))
        key_tiles = (key_count + TK - 1) // TK
        lax.fori_loop(0, key_tiles, functools.partial(project, patch, key_count), 0)
        steps = (query_count + TQ - 1) // TQ
        for tiles in range(1, PATCH_ROWS // TK + 1):

            @pl.when(key_tiles == tiles)
            def _():
                lax.fori_loop(0, steps, functools.partial(attend, tiles * TK), 0)

        lax.fori_loop(0, (query_count + TM - 1) // TM, functools.partial(finish, patch), 0)
        return carry

    lax.fori_loop(0, 2, one_patch, 0)

    def unpack(slot, carry):
        label = own_labels[slot, 0]

        @pl.when(label > 0)
        def _():
            rows = take_rows(packed.at[label // 64], offsets[slot])
            send[slot] = rows.astype(jnp.bfloat16)

        return carry

    lax.fori_loop(0, SLOTS, unpack, 0)


def return_kernel(slots, counts, send, out, arrived, send_sem, recv_sem):
    core = lax.axis_index("patch")
    meet()
    local = pltpu.make_async_copy(send.at[0], arrived.at[0], recv_sem.at[0])
    local.start()
    copies = []
    for offset in OFFSETS:
        slot = slot_number(offset)
        copy = pltpu.make_async_remote_copy(
            send.at[slot], arrived.at[slot], send_sem.at[slot], recv_sem.at[slot],
            device_id=(core, peer(offset, -1)), device_id_type=MESH,
        )
        copy.start()
        copies.append(copy)
    local.wait()
    for copy in copies:
        copy.wait()
    position = lax.broadcasted_iota(jnp.int32, (CELL, C), 0)
    for cell in range(CELLS_DEV):
        rows = arrived[slots[cell]].astype(jnp.float32)
        count = counts[cell // HALF_CELLS, cell % HALF_CELLS]
        out[cell] = jnp.where(position < count, rows, 0.0).astype(jnp.bfloat16)


def any_spec():
    return pl.BlockSpec(memory_space=pl.ANY)


def vmem_spec():
    return pl.BlockSpec(memory_space=pltpu.VMEM)


def smem_spec():
    return pl.BlockSpec(memory_space=pltpu.SMEM)


def shards(features, hilbert_rank, valid_count, norm_gains, w_qkv, w_out, w_up, w_down):
    slab = jax.ShapeDtypeStruct((SLOTS, CELL, C), jnp.bfloat16)
    label_shape = jax.ShapeDtypeStruct((SLOTS, 1, 128), jnp.int32)
    dma = pltpu.SemaphoreType.DMA
    send, labels, slots = pl.pallas_call(
        first_kernel,
        out_shape=(slab, label_shape, jax.ShapeDtypeStruct((CELLS_DEV,), jnp.int32)),
        in_specs=[smem_spec(), smem_spec(), vmem_spec(), vmem_spec(), any_spec(), any_spec()],
        out_specs=(vmem_spec(), vmem_spec(), smem_spec()),
        scratch_shapes=[
            pltpu.VMEM((CELLS_DEV * CELL + TM, C), jnp.float32),
            pltpu.VMEM((C, FF), jnp.bfloat16),
            pltpu.VMEM((FF, C), jnp.bfloat16),
            pltpu.SMEM((CELLS_DEV,), jnp.int32),
            pltpu.SMEM((SLOTS,), jnp.int32),
            dma((2,)),
        ],
        compiler_params=pltpu.CompilerParams(vmem_limit_bytes=VMEM_LIMIT),
        name="first",
    )(hilbert_rank, valid_count, features.reshape(CELLS_DEV * CELL, C), norm_gains, w_up, w_down)

    own, other, own_labels, other_labels = pl.pallas_call(
        forward_kernel,
        out_shape=(slab, slab, label_shape, label_shape),
        in_specs=[any_spec(), vmem_spec()],
        out_specs=(any_spec(), any_spec(), any_spec(), any_spec()),
        scratch_shapes=[
            pltpu.VMEM((SLOTS, CELL, C), jnp.bfloat16),
            pltpu.VMEM((SLOTS, 1, 128), jnp.int32),
            dma((SLOTS,)), dma((SLOTS,)), dma((SLOTS,)), dma((SLOTS,)),
            dma((SLOTS,)), dma((SLOTS,)), dma((SLOTS,)), dma((3,)),
        ],
        compiler_params=pltpu.CompilerParams(
            collective_id=0, has_side_effects=True, vmem_limit_bytes=VMEM_LIMIT
        ),
        name="forward",
    )(send, labels)

    send = pl.pallas_call(
        layer_kernel,
        out_shape=slab,
        in_specs=[smem_spec(), smem_spec(), vmem_spec(), vmem_spec(), vmem_spec()]
        + [any_spec()] * 4,
        out_specs=vmem_spec(),
        scratch_shapes=[
            pltpu.VMEM((2, PATCH_ROWS + 2 * TK, C), jnp.float32),
            pltpu.VMEM((GROUPS, PATCH_ROWS, GROUP_LANES), jnp.bfloat16),
            pltpu.VMEM((GROUPS, PATCH_ROWS, GROUP_LANES), jnp.bfloat16),
            pltpu.VMEM((GROUPS, GROUP_LANES + DEPTH, PATCH_ROWS), jnp.bfloat16),
            pltpu.VMEM((HALF_ROWS, C), jnp.bfloat16),
            pltpu.VMEM((C, 3 * C), jnp.bfloat16),
            pltpu.VMEM((C, C), jnp.bfloat16),
            pltpu.VMEM((C, FF), jnp.bfloat16),
            pltpu.VMEM((FF, C), jnp.bfloat16),
            pltpu.SMEM((SLOTS,), jnp.int32),
            dma((4,)),
        ],
        compiler_params=pltpu.CompilerParams(vmem_limit_bytes=VMEM_LIMIT),
        name="layer",
    )(
        own_labels.reshape(SLOTS, 128), other_labels.reshape(SLOTS, 128), own, other, norm_gains,
        w_qkv, w_out, w_up, w_down,
    )

    out = pl.pallas_call(
        return_kernel,
        out_shape=jax.ShapeDtypeStruct((CELLS_DEV, CELL, C), jnp.bfloat16),
        in_specs=[smem_spec(), smem_spec(), any_spec()],
        out_specs=vmem_spec(),
        scratch_shapes=[
            pltpu.VMEM((SLOTS, CELL, C), jnp.bfloat16),
            dma((SLOTS,)), dma((SLOTS,)),
        ],
        compiler_params=pltpu.CompilerParams(
            collective_id=1, has_side_effects=True, vmem_limit_bytes=VMEM_LIMIT
        ),
        name="homeward",
    )(slots, valid_count, send)
    return out.reshape(features.shape)


def solution(mesh):
    in_specs = (
        P("cells", "patch", None),
        P("cells", "patch"),
        P("cells", "patch"),
        P(),
        P(),
        P(),
        P(),
        P(),
    )
    out_specs = P("cells", "patch", None)
    return jax.shard_map(shards, mesh=mesh, in_specs=in_specs, out_specs=out_specs, check_vma=False)
```

```python
import functools
import itertools
import random

import jax
import jax.numpy as jnp
from jax import lax
from jax.experimental import pallas as pl
from jax.experimental.pallas import tpu as pltpu
from jax.sharding import PartitionSpec as P

MESH = pl.DeviceIdType.MESH
EPSILON = 1e-05
C = 512
FF = 2048
CELL = 32
SIDE = 4
SLOTS = SIDE**3
CELLS_DEV = 32
HALF_CELLS = 16
HALF_ROWS = 512
PATCH_ROWS = 1024
GROUPS = 4
GROUP_LANES = 128
GROUP_HEADS = 8
DEPTH = 16
TM = 128
TQ = 32
TK = 128
STACK = GROUP_HEADS * TQ
VMEM_LIMIT = 60 * 1024 * 1024

OFFSETS = [o for o in itertools.product(range(SIDE), repeat=3) if o != (0, 0, 0)]
random.Random(0).shuffle(OFFSETS)
OFFSETS = [(0, 0, 0)] + OFFSETS
BATCH = 4
BATCHES = SLOTS // BATCH


def number(offset):
    return (offset[0] * SIDE + offset[1]) * SIDE + offset[2]


def coordinates():
    me = lax.axis_index("cells")
    return me // (SIDE * SIDE), (me // SIDE) % SIDE, me % SIDE


def peer(offset, sign):
    y, x, z = coordinates()
    ys = (y + sign * offset[0] + SIDE) % SIDE
    xs = (x + sign * offset[1] + SIDE) % SIDE
    zs = (z + sign * offset[2] + SIDE) % SIDE
    return (ys * SIDE + xs) * SIDE + zs


def norm_rows(values, gains):
    center = values - jnp.mean(values, axis=-1, keepdims=True)
    spread = jnp.mean(center * center, axis=-1, keepdims=True)
    return (center * lax.rsqrt(spread + EPSILON) * gains).astype(jnp.bfloat16)


def mlp_rows(rows, gain_row, w_up, w_down):
    normed = norm_rows(rows, gain_row)
    raised = jnp.dot(normed, w_up, preferred_element_type=jnp.float32)
    hidden = jax.nn.gelu(raised, approximate=True).astype(jnp.bfloat16)
    return rows + jnp.dot(hidden, w_down, preferred_element_type=jnp.float32)


def put_rows(ref, start, rows):
    base = pl.multiple_of((start >> 3) << 3, 8)
    shift = start - base
    padded = jnp.concatenate([rows, jnp.zeros((8, C), jnp.float32)], axis=0)
    moved = pltpu.roll(padded, shift, 0)
    position = lax.broadcasted_iota(jnp.int32, (8, C), 0)
    pltpu.store(ref.at[pl.ds(base, 8), :], moved[:8], mask=position >= shift)
    ref[pl.ds(pl.multiple_of(base + 8, 8), CELL), :] = moved[8:]


def take_rows(ref, start):
    base = pl.multiple_of((start >> 3) << 3, 8)
    window = ref[pl.ds(base, CELL + 8), :]
    ahead = start - base
    return pltpu.roll(window, jnp.where(ahead == 0, 0, CELL + 8 - ahead), 0)[:CELL]


def table_kernel(rank_ref, count_ref, cell_of, labels, slots, place, label_of, found):
    me = lax.axis_index("cells")
    y, x, z = me >> 4, (me >> 2) & 3, me & 3
    for slot, offset in enumerate(OFFSETS):
        place[number(offset)] = slot
        label_of[slot] = 0
        found[slot] = 0

    def one(cell, carry):
        rank = rank_ref[cell >> 4, cell & 15]
        owner = rank >> 6
        oy = ((owner >> 4) - y) & 3
        ox = (((owner >> 2) & 3) - x) & 3
        oz = ((owner & 3) - z) & 3
        slot = place[(oy << 4) | (ox << 2) | oz]
        slots[cell] = slot
        found[slot] = cell
        label_of[slot] = count_ref[cell >> 4, cell & 15] + 64 * ((rank >> 5) & 1)
        return carry

    lax.fori_loop(0, CELLS_DEV, one, 0)
    for slot in range(SLOTS):
        cell_of[slot] = found[slot]
        labels[slot] = jnp.full((1, 128), label_of[slot], jnp.int32)


def meet():
    core = lax.axis_index("patch")
    barrier = pltpu.get_barrier_semaphore()
    for offset in OFFSETS[1:]:
        pl.semaphore_signal(barrier, inc=1, device_id=(core, peer(offset, 1)), device_id_type=MESH)
    pl.semaphore_signal(
        barrier, inc=1, device_id=(1 - core, lax.axis_index("cells")), device_id_type=MESH
    )
    return barrier


def batch_mlp(batch, arrived, done, gain_row, w_up, w_down):
    slots = pl.ds(pl.multiple_of(batch * BATCH, BATCH), BATCH)
    rows = arrived[slots].reshape(BATCH * CELL, C).astype(jnp.float32)
    rows = mlp_rows(rows, gain_row, w_up[...], w_down[...])
    done[slots] = rows.astype(jnp.bfloat16).reshape(BATCH, CELL, C)


def forward_kernel(
    cell_of, labels, features, gains, up_hbm, down_hbm, own, other, own_labels, other_labels,
    send, arrived, arrived_labels, done, w_up, w_down,
    send_sem, recv_sem, label_send, label_recv, keep_sem, pass_sem, got_sem, tail_sem, sems,
):
    core = lax.axis_index("patch")
    sibling = (1 - core, lax.axis_index("cells"))
    barrier = meet()
    weights = [
        pltpu.make_async_copy(up_hbm.at[0], w_up, sems.at[0]),
        pltpu.make_async_copy(down_hbm.at[0], w_down, sems.at[1]),
    ]
    for copy in weights:
        copy.start()
    for slot in range(SLOTS):
        send[slot] = features[cell_of[slot]]
    pl.semaphore_wait(barrier, SLOTS)

    label_copies = [
        pltpu.make_async_copy(labels.at[0], arrived_labels.at[0], label_recv.at[0])
    ]
    copies = [pltpu.make_async_copy(send.at[0], arrived.at[0], recv_sem.at[0])]
    for slot, offset in enumerate(OFFSETS):
        to = (core, peer(offset, 1))
        if slot > 0:
            copies.append(
                pltpu.make_async_remote_copy(
                    send.at[slot], arrived.at[slot], send_sem.at[slot], recv_sem.at[slot],
                    device_id=to, device_id_type=MESH,
                )
            )
            label_copies.append(
                pltpu.make_async_remote_copy(
                    labels.at[slot], arrived_labels.at[slot],
                    label_send.at[slot], label_recv.at[slot],
                    device_id=to, device_id_type=MESH,
                )
            )
        copies[slot].start()
        label_copies[slot].start()
    for copy in weights:
        copy.wait()

    def step(batch, carry):
        for index in range(BATCH):
            slot = batch * BATCH + index
            pltpu.make_async_copy(send.at[slot], arrived.at[slot], recv_sem.at[slot]).wait()
        batch_mlp(batch, arrived, done, gains[0:1, :], w_up, w_down)
        slots = pl.ds(pl.multiple_of(batch * BATCH, BATCH), BATCH)
        pltpu.make_async_copy(done.at[slots], own.at[slots], keep_sem.at[batch]).start()
        pltpu.make_async_remote_copy(
            done.at[slots], other.at[slots], pass_sem.at[batch], got_sem.at[batch],
            device_id=sibling, device_id_type=MESH,
        ).start()
        return carry

    lax.fori_loop(0, BATCHES, step, 0)
    for slot, copy in enumerate(label_copies):
        if slot == 0:
            copy.wait()
        else:
            copy.wait_recv()
    keep_labels = pltpu.make_async_copy(arrived_labels, own_labels, tail_sem.at[0])
    pass_labels = pltpu.make_async_remote_copy(
        arrived_labels, other_labels, tail_sem.at[1], tail_sem.at[2],
        device_id=sibling, device_id_type=MESH,
    )
    keep_labels.start()
    pass_labels.start()
    for copy in copies[1:]:
        copy.wait_send()
    for copy in label_copies[1:]:
        copy.wait_send()

    def drain(batch, carry):
        slots = pl.ds(pl.multiple_of(batch * BATCH, BATCH), BATCH)
        pltpu.make_async_copy(done.at[slots], own.at[slots], keep_sem.at[batch]).wait()
        pltpu.make_async_remote_copy(
            done.at[slots], other.at[slots], pass_sem.at[batch], got_sem.at[batch],
            device_id=sibling, device_id_type=MESH,
        ).wait()
        return carry

    lax.fori_loop(0, BATCHES, drain, 0)
    keep_labels.wait()
    pass_labels.wait()


def layer_kernel(
    own_labels, other_labels, own, other, gains, qkv_hbm, out_hbm,
    send, packed, queries, keys, values, mixed, w_qkv, w_out, offsets, filled, sems,
):
    copies = [
        pltpu.make_async_copy(qkv_hbm, w_qkv, sems.at[0]),
        pltpu.make_async_copy(out_hbm, w_out, sems.at[1]),
    ]
    for copy in copies:
        copy.start()

    def pack(labels, cells, starts):
        count = jnp.int32(0)
        for slot in range(SLOTS):
            filled[count] = slot
            count = count + jnp.where(labels[slot, 0] > 0, 1, 0)

        def one(cell, starts):
            slot = filled[cell]
            label = labels[slot, 0]
            patch = label >> 6
            count = label & 63
            start = jnp.where(patch == 0, starts[0], starts[1])
            if labels is own_labels:
                offsets[cell] = start
            put_rows(packed.at[patch], start, cells[slot].astype(jnp.float32))
            first = jnp.where(patch == 0, count, 0)
            return starts[0] + first, starts[1] + count - first

        return lax.fori_loop(0, CELLS_DEV, one, starts, unroll=4)

    pack_own = functools.partial(pack, own_labels, own)
    pack_other = functools.partial(pack, other_labels, other)
    query_rows = pack_own((jnp.int32(0), jnp.int32(0)))
    key_rows = pack_other(query_rows)
    for copy in copies:
        copy.wait()
    lane = lax.broadcasted_iota(jnp.int32, (1, GROUP_LANES), 1) // DEPTH
    head_masks = [(lane == head).astype(jnp.float32) for head in range(GROUP_HEADS)]

    def project(patch, key_count, step, carry):
        base = pl.multiple_of(step * TM, TM)
        rows = pl.ds(base, TM)
        normed = norm_rows(packed[patch, rows, :], gains[1:2, :])
        projected = jnp.dot(normed, w_qkv[...], preferred_element_type=jnp.float32)
        projected = projected.astype(jnp.bfloat16)
        seen = lax.broadcasted_iota(jnp.int32, (GROUP_LANES, TM), 1) + base < key_count
        ones = lax.broadcasted_iota(jnp.int32, (DEPTH, TM), 1) + base < key_count
        for group in range(GROUPS):
            low = group * GROUP_LANES
            queries[group, rows, :] = projected[:, low : low + GROUP_LANES] * 0.25
            keys[group, rows, :] = projected[:, C + low : C + low + GROUP_LANES]
            value = projected[:, 2 * C + low : 2 * C + low + GROUP_LANES].astype(jnp.float32)
            values[group, :GROUP_LANES, rows] = jnp.where(seen, value.T, 0.0).astype(jnp.bfloat16)
            values[group, GROUP_LANES:, rows] = jnp.where(ones, 1.0, 0.0).astype(jnp.bfloat16)
        return carry

    fold = lax.broadcasted_iota(jnp.int32, (TQ, STACK), 1) % TQ
    fold = fold == lax.broadcasted_iota(jnp.int32, (TQ, STACK), 0)
    fold = fold.astype(jnp.float32).astype(jnp.bfloat16)
    block = lax.broadcasted_iota(jnp.int32, (GROUP_LANES, STACK), 0) // DEPTH
    block = block == lax.broadcasted_iota(jnp.int32, (GROUP_LANES, STACK), 1) // TQ

    def attend(key_span, step, carry):
        rows = pl.ds(pl.multiple_of(step * TQ, TQ), TQ)

        def score(group):
            query = queries[group, rows, :].astype(jnp.float32)
            stacked = jnp.concatenate([query * mask for mask in head_masks], axis=0)
            return lax.dot_general(
                keys[group, :key_span, :], stacked.astype(jnp.bfloat16),
                (((1,), (1,)), ((), ())), preferred_element_type=jnp.float32,
            )

        def weigh(scores):
            highest = jnp.max(scores, axis=0, keepdims=True)
            return jnp.exp(scores - highest).astype(jnp.bfloat16)

        def mix(group, weights):
            mixture = jnp.dot(
                values[group, :, :key_span], weights, preferred_element_type=jnp.float32
            )
            top = mixture[:GROUP_LANES] / mixture[GROUP_LANES : GROUP_LANES + 1]
            return jnp.where(block, top, 0.0).astype(jnp.bfloat16)

        def store(group, top):
            low = group * GROUP_LANES
            mixed[rows, low : low + GROUP_LANES] = lax.dot_general(
                fold, top, (((1,), (1,)), ((), ())), preferred_element_type=jnp.float32
            ).astype(jnp.bfloat16)

        scores = [score(group) for group in range(GROUPS)]
        weights = [weigh(value) for value in scores]
        tops = [mix(group, value) for group, value in enumerate(weights)]
        for group, top in enumerate(tops):
            store(group, top)
        return carry

    def finish(patch, step, carry):
        rows = pl.ds(pl.multiple_of(step * TM, TM), TM)
        middle = packed[patch, rows, :] + jnp.dot(
            mixed[rows, :], w_out[...], preferred_element_type=jnp.float32
        )
        packed[patch, rows, :] = middle
        return carry

    def one_patch(patch, carry):
        query_count = jnp.where(patch == 0, query_rows[0], query_rows[1])
        key_count = jnp.where(patch == 0, key_rows[0], key_rows[1])
        base = pl.multiple_of(key_count // 8 * 8, 8)
        spare = jnp.broadcast_to(packed[patch, 0:1, :], (8, C))
        edge = packed[patch, pl.ds(base, 8), :]
        position = lax.broadcasted_iota(jnp.int32, (8, C), 0)
        packed[patch, pl.ds(base, 8), :] = jnp.where(position < key_count - base, edge, spare)
        packed[patch, pl.ds(pl.multiple_of(base + 8, 8), TK), :] = jnp.broadcast_to(spare[:1], (TK, C))
        key_tiles = (key_count + TK - 1) // TK
        lax.fori_loop(0, key_tiles, functools.partial(project, patch, key_count), 0)
        steps = (query_count + TQ - 1) // TQ
        for tiles in range(1, PATCH_ROWS // TK + 1):

            @pl.when(key_tiles == tiles)
            def _():
                lax.fori_loop(0, steps, functools.partial(attend, tiles * TK), 0)

        lax.fori_loop(0, (query_count + TM - 1) // TM, functools.partial(finish, patch), 0)
        return carry

    lax.fori_loop(0, 2, one_patch, 0)

    count = jnp.int32(0)
    for slot in range(SLOTS):
        filled[count] = slot
        count = count + jnp.where(own_labels[slot, 0] > 0, 1, 0)

    def unpack(cell, carry):
        slot = filled[cell]
        rows = take_rows(packed.at[own_labels[slot, 0] >> 6], offsets[cell])
        send[slot] = rows.astype(jnp.bfloat16)
        return carry

    lax.fori_loop(0, CELLS_DEV, unpack, 0, unroll=4)


def return_kernel(
    slots, counts, send, gains, up_hbm, down_hbm, out,
    arrived, done, w_up, w_down, send_sem, recv_sem, sems,
):
    core = lax.axis_index("patch")
    barrier = meet()
    weights = [
        pltpu.make_async_copy(up_hbm.at[1], w_up, sems.at[0]),
        pltpu.make_async_copy(down_hbm.at[1], w_down, sems.at[1]),
    ]
    for copy in weights:
        copy.start()
    pl.semaphore_wait(barrier, SLOTS)
    copies = [pltpu.make_async_copy(send.at[0], arrived.at[0], recv_sem.at[0])]
    copies[0].start()
    for slot, offset in enumerate(OFFSETS):
        if slot > 0:
            copy = pltpu.make_async_remote_copy(
                send.at[slot], arrived.at[slot], send_sem.at[slot], recv_sem.at[slot],
                device_id=(core, peer(offset, -1)), device_id_type=MESH,
            )
            copy.start()
            copies.append(copy)
    for copy in weights:
        copy.wait()

    def step(batch, carry):
        for index in range(BATCH):
            slot = batch * BATCH + index
            pltpu.make_async_copy(send.at[slot], arrived.at[slot], recv_sem.at[slot]).wait()
        batch_mlp(batch, arrived, done, gains[2:3, :], w_up, w_down)
        return carry

    lax.fori_loop(0, BATCHES, step, 0)
    for copy in copies[1:]:
        copy.wait_send()
    position = lax.broadcasted_iota(jnp.int32, (CELL, C), 0)
    for cell in range(CELLS_DEV):
        rows = done[slots[cell]].astype(jnp.float32)
        count = counts[cell // HALF_CELLS, cell % HALF_CELLS]
        out[cell] = jnp.where(position < count, rows, 0.0).astype(jnp.bfloat16)


def any_spec():
    return pl.BlockSpec(memory_space=pl.ANY)


def vmem_spec():
    return pl.BlockSpec(memory_space=pltpu.VMEM)


def smem_spec():
    return pl.BlockSpec(memory_space=pltpu.SMEM)


def shards(features, hilbert_rank, valid_count, norm_gains, w_qkv, w_out, w_up, w_down):
    slab = jax.ShapeDtypeStruct((SLOTS, CELL, C), jnp.bfloat16)
    label_shape = jax.ShapeDtypeStruct((SLOTS, 1, 128), jnp.int32)
    dma = pltpu.SemaphoreType.DMA
    slab_vmem = pltpu.VMEM((SLOTS, CELL, C), jnp.bfloat16)
    up_vmem = pltpu.VMEM((C, FF), jnp.bfloat16)
    down_vmem = pltpu.VMEM((FF, C), jnp.bfloat16)
    cell_of, labels, slots = pl.pallas_call(
        table_kernel,
        out_shape=(
            jax.ShapeDtypeStruct((SLOTS,), jnp.int32),
            label_shape,
            jax.ShapeDtypeStruct((CELLS_DEV,), jnp.int32),
        ),
        in_specs=[smem_spec(), smem_spec()],
        out_specs=(smem_spec(), vmem_spec(), smem_spec()),
        scratch_shapes=[
            pltpu.SMEM((SLOTS,), jnp.int32),
            pltpu.SMEM((SLOTS,), jnp.int32),
            pltpu.SMEM((SLOTS,), jnp.int32),
        ],
        name="tables",
    )(hilbert_rank, valid_count)

    own, other, own_labels, other_labels = pl.pallas_call(
        forward_kernel,
        out_shape=(slab, slab, label_shape, label_shape),
        in_specs=[smem_spec(), vmem_spec(), vmem_spec(), vmem_spec(), any_spec(), any_spec()],
        out_specs=(any_spec(), any_spec(), any_spec(), any_spec()),
        scratch_shapes=[
            slab_vmem, slab_vmem, pltpu.VMEM((SLOTS, 1, 128), jnp.int32), slab_vmem,
            up_vmem, down_vmem,
            dma((SLOTS,)), dma((SLOTS,)), dma((SLOTS,)), dma((SLOTS,)),
            dma((BATCHES,)), dma((BATCHES,)), dma((BATCHES,)), dma((3,)), dma((2,)),
        ],
        compiler_params=pltpu.CompilerParams(
            collective_id=0, has_side_effects=True, vmem_limit_bytes=VMEM_LIMIT
        ),
        name="forward",
    )(cell_of, labels, features.reshape(CELLS_DEV, CELL, C), norm_gains, w_up, w_down)

    send = pl.pallas_call(
        layer_kernel,
        out_shape=slab,
        in_specs=[smem_spec(), smem_spec(), vmem_spec(), vmem_spec(), vmem_spec()]
        + [any_spec()] * 2,
        out_specs=vmem_spec(),
        scratch_shapes=[
            pltpu.VMEM((2, PATCH_ROWS + 2 * TK, C), jnp.float32),
            pltpu.VMEM((GROUPS, PATCH_ROWS, GROUP_LANES), jnp.bfloat16),
            pltpu.VMEM((GROUPS, PATCH_ROWS, GROUP_LANES), jnp.bfloat16),
            pltpu.VMEM((GROUPS, GROUP_LANES + DEPTH, PATCH_ROWS), jnp.bfloat16),
            pltpu.VMEM((HALF_ROWS, C), jnp.bfloat16),
            pltpu.VMEM((C, 3 * C), jnp.bfloat16),
            pltpu.VMEM((C, C), jnp.bfloat16),
            pltpu.SMEM((CELLS_DEV,), jnp.int32),
            pltpu.SMEM((SLOTS + 1,), jnp.int32),
            dma((2,)),
        ],
        compiler_params=pltpu.CompilerParams(vmem_limit_bytes=VMEM_LIMIT),
        name="layer",
    )(
        own_labels.reshape(SLOTS, 128), other_labels.reshape(SLOTS, 128), own, other, norm_gains,
        w_qkv, w_out,
    )

    out = pl.pallas_call(
        return_kernel,
        out_shape=jax.ShapeDtypeStruct((CELLS_DEV, CELL, C), jnp.bfloat16),
        in_specs=[smem_spec(), smem_spec(), any_spec(), vmem_spec(), any_spec(), any_spec()],
        out_specs=vmem_spec(),
        scratch_shapes=[
            slab_vmem, slab_vmem, up_vmem, down_vmem, dma((SLOTS,)), dma((SLOTS,)), dma((2,)),
        ],
        compiler_params=pltpu.CompilerParams(
            collective_id=1, has_side_effects=True, vmem_limit_bytes=VMEM_LIMIT
        ),
        name="homeward",
    )(slots, valid_count, send, norm_gains, w_up, w_down)
    return out.reshape(features.shape)


def solution(mesh):
    in_specs = (
        P("cells", "patch", None),
        P("cells", "patch"),
        P("cells", "patch"),
        P(),
        P(),
        P(),
        P(),
        P(),
    )
    out_specs = P("cells", "patch", None)
    return jax.shard_map(shards, mesh=mesh, in_specs=in_specs, out_specs=out_specs, check_vma=False)
```

```python
import functools
import itertools
import math
import random

import jax
import jax.numpy as jnp
from jax import lax
from jax.experimental import pallas as pl
from jax.experimental.pallas import tpu as pltpu
from jax.sharding import PartitionSpec as P

MESH = pl.DeviceIdType.MESH
EPSILON = 1e-05
C = 512
FF = 2048
CELL = 32
SIDE = 4
SLOTS = SIDE**3
CELLS_DEV = 32
HALF_CELLS = 16
HALF_ROWS = 512
PATCH_ROWS = 1024
GROUPS = 4
GROUP_LANES = 128
GROUP_HEADS = 8
DEPTH = 16
GELU_LINEAR = math.sqrt(2 / math.pi)
GELU_CUBIC = 0.044715 * GELU_LINEAR
QUERY_SCALE = DEPTH**-0.5 * math.log2(math.e)
TM = 128
TQ = 32
TK = 128
STACK = GROUP_HEADS * TQ
VMEM_LIMIT = 60 * 1024 * 1024

OFFSETS = [o for o in itertools.product(range(SIDE), repeat=3) if o != (0, 0, 0)]
random.Random(0).shuffle(OFFSETS)
OFFSETS = [(0, 0, 0)] + OFFSETS
BATCH = 4
BATCHES = SLOTS // BATCH


def number(offset):
    return (offset[0] * SIDE + offset[1]) * SIDE + offset[2]


def peers(sign):
    me = lax.axis_index("cells")
    ys = [lax.rem(lax.div(me, 16) + d, SIDE) * 16 for d in range(SIDE)]
    xs = [lax.rem(lax.div(me, 4) + d, SIDE) * 4 for d in range(SIDE)]
    zs = [lax.rem(me + d, SIDE) for d in range(SIDE)]
    return [
        ys[sign * oy % SIDE] + xs[sign * ox % SIDE] + zs[sign * oz % SIDE]
        for oy, ox, oz in OFFSETS
    ]


def norm_rows(values, gains):
    center = values - jnp.mean(values, axis=-1, keepdims=True)
    spread = jnp.mean(center * center, axis=-1, keepdims=True)
    return (center * lax.rsqrt(spread + EPSILON) * gains).astype(jnp.bfloat16)


def gelu(value):
    inner = value * (GELU_LINEAR + GELU_CUBIC * (value * value))
    half = 0.5 * value
    return (half + half * jnp.tanh(inner)).astype(jnp.bfloat16)


def mlp_rows(rows, gain_row, w_up, w_down):
    normed = norm_rows(rows, gain_row)
    raised = jnp.dot(normed, w_up[...], preferred_element_type=jnp.float32)
    return rows + jnp.dot(gelu(raised), w_down[...], preferred_element_type=jnp.float32)


def put_rows(ref, start, rows):
    base = pl.multiple_of((start >> 3) << 3, 8)
    shift = start - base
    padded = jnp.concatenate([rows, jnp.zeros((8, C), jnp.float32)], axis=0)
    moved = pltpu.roll(padded, shift, 0)
    position = lax.broadcasted_iota(jnp.int32, (8, C), 0)
    pltpu.store(ref.at[pl.ds(base, 8), :], moved[:8], mask=position >= shift)
    ref[pl.ds(pl.multiple_of(base + 8, 8), CELL), :] = moved[8:]


def take_rows(ref, start):
    base = pl.multiple_of((start >> 3) << 3, 8)
    window = ref[pl.ds(base, CELL + 8), :]
    ahead = start - base
    return pltpu.roll(window, jnp.where(ahead == 0, 0, CELL + 8 - ahead), 0)[:CELL]


def table_kernel(rank_ref, count_ref, cell_of, labels, slots, place, label_of, found):
    me = lax.axis_index("cells")
    y, x, z = me >> 4, (me >> 2) & 3, me & 3
    for slot, offset in enumerate(OFFSETS):
        place[number(offset)] = slot
        label_of[slot] = 0
        found[slot] = 0

    def one(cell, carry):
        rank = rank_ref[cell >> 4, cell & 15]
        owner = rank >> 6
        oy = ((owner >> 4) - y) & 3
        ox = (((owner >> 2) & 3) - x) & 3
        oz = ((owner & 3) - z) & 3
        slot = place[(oy << 4) | (ox << 2) | oz]
        slots[cell] = slot
        found[slot] = cell
        label_of[slot] = count_ref[cell >> 4, cell & 15] + 64 * ((rank >> 5) & 1)
        return carry

    lax.fori_loop(0, CELLS_DEV, one, 0)
    for slot in range(SLOTS):
        cell_of[slot] = found[slot]
        labels[slot] = jnp.full((1, 128), label_of[slot], jnp.int32)


def meet(others):
    core = lax.axis_index("patch")
    barrier = pltpu.get_barrier_semaphore()
    for other in others[1:]:
        pl.semaphore_signal(barrier, inc=1, device_id=(core, other), device_id_type=MESH)
    pl.semaphore_signal(
        barrier, inc=1, device_id=(1 - core, lax.axis_index("cells")), device_id_type=MESH
    )
    return barrier


def batch_mlp(batch, arrived, done, gain_row, w_up, w_down):
    slots = pl.ds(pl.multiple_of(batch * BATCH, BATCH), BATCH)
    rows = arrived[slots].reshape(BATCH * CELL, C).astype(jnp.float32)
    rows = mlp_rows(rows, gain_row, w_up, w_down)
    done[slots] = rows.astype(jnp.bfloat16).reshape(BATCH, CELL, C)


def forward_kernel(
    cell_of, labels, features, gains, up_hbm, down_hbm, own, other, own_labels, other_labels,
    send, arrived, arrived_labels, done, w_up, w_down,
    send_sem, recv_sem, label_send, label_recv, keep_sem, pass_sem, got_sem, tail_sem, sems,
):
    core = lax.axis_index("patch")
    sibling = (1 - core, lax.axis_index("cells"))
    others = peers(1)
    barrier = meet(others)
    weights = [
        pltpu.make_async_copy(up_hbm.at[0], w_up, sems.at[0]),
        pltpu.make_async_copy(down_hbm.at[0], w_down, sems.at[1]),
    ]
    for copy in weights:
        copy.start()
    for slot in range(SLOTS):
        send[slot] = features[cell_of[slot]]
    pl.semaphore_wait(barrier, SLOTS)

    pltpu.make_async_copy(send.at[0], arrived.at[0], recv_sem.at[0]).start()
    local_labels = pltpu.make_async_copy(labels.at[0], arrived_labels.at[0], tail_sem.at[3])
    local_labels.start()
    for slot in range(1, SLOTS):
        pltpu.make_async_remote_copy(
            send.at[slot], arrived.at[slot], send_sem, recv_sem.at[slot],
            device_id=(core, others[slot]), device_id_type=MESH,
        ).start()
    for slot in range(1, SLOTS):
        pltpu.make_async_remote_copy(
            labels.at[slot], arrived_labels.at[slot], label_send, label_recv,
            device_id=(core, others[slot]), device_id_type=MESH,
        ).start()
    for copy in weights:
        copy.wait()

    def step(batch, carry):
        for index in range(BATCH):
            slot = batch * BATCH + index
            pltpu.make_async_copy(send.at[slot], arrived.at[slot], recv_sem.at[slot]).wait()
        batch_mlp(batch, arrived, done, gains[0:1, :], w_up, w_down)
        slots = pl.ds(pl.multiple_of(batch * BATCH, BATCH), BATCH)
        pltpu.make_async_copy(done.at[slots], own.at[slots], keep_sem.at[batch]).start()
        pltpu.make_async_remote_copy(
            done.at[slots], other.at[slots], pass_sem.at[batch], got_sem.at[batch],
            device_id=sibling, device_id_type=MESH,
        ).start()
        return carry

    lax.fori_loop(0, BATCHES, step, 0)
    remote = pl.ds(1, SLOTS - 1)
    all_labels = pltpu.make_async_remote_copy(
        labels.at[remote], arrived_labels.at[remote], label_send, label_recv,
        device_id=sibling, device_id_type=MESH,
    )
    all_labels.wait_recv()
    local_labels.wait()
    keep_labels = pltpu.make_async_copy(arrived_labels, own_labels, tail_sem.at[0])
    pass_labels = pltpu.make_async_remote_copy(
        arrived_labels, other_labels, tail_sem.at[1], tail_sem.at[2],
        device_id=sibling, device_id_type=MESH,
    )
    keep_labels.start()
    pass_labels.start()
    all_labels.wait_send()
    pltpu.make_async_remote_copy(
        send.at[remote], arrived.at[remote], send_sem, recv_sem.at[0],
        device_id=sibling, device_id_type=MESH,
    ).wait_send()

    def drain(batch, carry):
        slots = pl.ds(pl.multiple_of(batch * BATCH, BATCH), BATCH)
        pltpu.make_async_copy(done.at[slots], own.at[slots], keep_sem.at[batch]).wait()
        pltpu.make_async_remote_copy(
            done.at[slots], other.at[slots], pass_sem.at[batch], got_sem.at[batch],
            device_id=sibling, device_id_type=MESH,
        ).wait()
        return carry

    lax.fori_loop(0, BATCHES, drain, 0)
    keep_labels.wait()
    pass_labels.wait()


def layer_kernel(
    own_labels, other_labels, own, other, gains, qkv_hbm, out_hbm,
    send, packed, queries, keys, values, mixed, ahead, w_qkv, w_out, offsets, own_filled, other_filled, sems,
):
    copies = [
        pltpu.make_async_copy(qkv_hbm, w_qkv, sems.at[0]),
        pltpu.make_async_copy(out_hbm, w_out, sems.at[1]),
    ]
    for copy in copies:
        copy.start()

    def pack(labels, cells, filled, starts):
        count = jnp.int32(0)
        for slot in range(SLOTS):
            filled[count] = slot
            count = count + jnp.where(labels[slot, 0] > 0, 1, 0)

        def one(cell, starts):
            slot = filled[cell]
            label = labels[slot, 0]
            patch = label >> 6
            count = label & 63
            start = jnp.where(patch == 0, starts[0], starts[1])
            if labels is own_labels:
                offsets[cell] = start
            put_rows(packed.at[patch], start, cells[slot].astype(jnp.float32))
            first = jnp.where(patch == 0, count, 0)
            return starts[0] + first, starts[1] + count - first

        return lax.fori_loop(0, CELLS_DEV, one, starts, unroll=4)

    pack_own = functools.partial(pack, own_labels, own, own_filled)
    pack_other = functools.partial(pack, other_labels, other, other_filled)
    query_rows = pack_own((jnp.int32(0), jnp.int32(0)))
    key_rows = pack_other(query_rows)
    for copy in copies:
        copy.wait()
    lane = lax.broadcasted_iota(jnp.int32, (1, GROUP_LANES), 1) // DEPTH
    head_masks = [(lane == head).astype(jnp.float32) for head in range(GROUP_HEADS)]

    def project(patch, key_count, step, carry):
        base = pl.multiple_of(step * TM, TM)
        rows = pl.ds(base, TM)
        normed = norm_rows(packed[patch, rows, :], gains[1:2, :])
        raw = jnp.dot(normed, w_qkv[...], preferred_element_type=jnp.float32)
        projected = raw.astype(jnp.bfloat16)
        seen = lax.broadcasted_iota(jnp.int32, (GROUP_LANES, TM), 1) + base < key_count
        ones = lax.broadcasted_iota(jnp.int32, (DEPTH, TM), 1) + base < key_count
        for group in range(GROUPS):
            low = group * GROUP_LANES
            query = raw[:, low : low + GROUP_LANES] * QUERY_SCALE
            queries[group, rows, :] = query.astype(jnp.bfloat16)
            keys[group, rows, :] = projected[:, C + low : C + low + GROUP_LANES]
            value = projected[:, 2 * C + low : 2 * C + low + GROUP_LANES].astype(jnp.float32)
            values[group, :GROUP_LANES, rows] = jnp.where(seen, value.T, 0.0).astype(jnp.bfloat16)
            values[group, GROUP_LANES:, rows] = jnp.where(ones, 1.0, 0.0).astype(jnp.bfloat16)
        return carry

    fold = lax.broadcasted_iota(jnp.int32, (TQ, STACK), 1) % TQ
    fold = fold == lax.broadcasted_iota(jnp.int32, (TQ, STACK), 0)
    fold = fold.astype(jnp.float32).astype(jnp.bfloat16)
    block = lax.broadcasted_iota(jnp.int32, (GROUP_LANES, STACK), 0) // DEPTH
    block = block == lax.broadcasted_iota(jnp.int32, (GROUP_LANES, STACK), 1) // TQ

    def score(group, key_span, tile):
        query = queries[group, pl.ds(pl.multiple_of(tile * TQ, TQ), TQ), :].astype(jnp.float32)
        stacked = jnp.concatenate([query * mask for mask in head_masks], axis=0)
        return lax.dot_general(
            keys[group, :key_span, :], stacked.astype(jnp.bfloat16),
            (((1,), (1,)), ((), ())), preferred_element_type=jnp.float32,
        )

    def weigh(scores):
        highest = jnp.max(scores, axis=0, keepdims=True)
        return jnp.exp2(scores - highest).astype(jnp.bfloat16)

    def mix(group, key_span, weights):
        mixture = jnp.dot(
            values[group, :, :key_span], weights, preferred_element_type=jnp.float32
        )
        top = mixture[:GROUP_LANES] / mixture[GROUP_LANES : GROUP_LANES + 1]
        return jnp.where(block, top, 0.0).astype(jnp.bfloat16)

    def attend(key_span, steps):
        ahead[0, :key_span, :] = score(0, key_span, 0)
        ahead[1, :key_span, :] = score(1, key_span, 0)

        def one(step, carry):
            rows = pl.ds(pl.multiple_of(step * TQ, TQ), TQ)
            following = jnp.minimum(step + 1, steps - 1)
            late = [score(2, key_span, step), score(3, key_span, step)]
            weights = [weigh(ahead[0, :key_span, :]), weigh(ahead[1, :key_span, :])]
            tops = [mix(group, key_span, weights[group]) for group in range(2)]
            early = [score(0, key_span, following), score(1, key_span, following)]
            weights = [weigh(value) for value in late]
            for group in range(2):
                ahead[group, :key_span, :] = early[group]
            tops += [mix(group + 2, key_span, weights[group]) for group in range(2)]
            for group, top in enumerate(tops):
                low = group * GROUP_LANES
                mixed[rows, low : low + GROUP_LANES] = lax.dot_general(
                    fold, top, (((1,), (1,)), ((), ())), preferred_element_type=jnp.float32
                ).astype(jnp.bfloat16)
            return carry

        lax.fori_loop(0, steps, one, 0)

    def finish(patch, step, carry):
        rows = pl.ds(pl.multiple_of(step * TM, TM), TM)
        middle = packed[patch, rows, :] + jnp.dot(
            mixed[rows, :], w_out[...], preferred_element_type=jnp.float32
        )
        packed[patch, rows, :] = middle
        return carry

    def one_patch(patch, carry):
        query_count = jnp.where(patch == 0, query_rows[0], query_rows[1])
        key_count = jnp.where(patch == 0, key_rows[0], key_rows[1])
        base = pl.multiple_of(key_count // 8 * 8, 8)
        spare = jnp.broadcast_to(packed[patch, 0:1, :], (8, C))
        edge = packed[patch, pl.ds(base, 8), :]
        position = lax.broadcasted_iota(jnp.int32, (8, C), 0)
        packed[patch, pl.ds(base, 8), :] = jnp.where(position < key_count - base, edge, spare)
        packed[patch, pl.ds(pl.multiple_of(base + 8, 8), TK), :] = jnp.broadcast_to(spare[:1], (TK, C))
        key_tiles = (key_count + TK - 1) // TK
        lax.fori_loop(0, key_tiles, functools.partial(project, patch, key_count), 0)
        steps = (query_count + TQ - 1) // TQ
        for tiles in range(1, PATCH_ROWS // TK + 1):

            @pl.when(key_tiles == tiles)
            def _():
                attend(tiles * TK, steps)

        lax.fori_loop(0, (query_count + TM - 1) // TM, functools.partial(finish, patch), 0)
        return carry

    lax.fori_loop(0, 2, one_patch, 0)

    def unpack(cell, carry):
        slot = own_filled[cell]
        rows = take_rows(packed.at[own_labels[slot, 0] >> 6], offsets[cell])
        send[slot] = rows.astype(jnp.bfloat16)
        return carry

    lax.fori_loop(0, CELLS_DEV, unpack, 0, unroll=4)


def return_kernel(
    slots, counts, send, gains, up_hbm, down_hbm, out,
    arrived, done, w_up, w_down, send_sem, recv_sem, sems,
):
    core = lax.axis_index("patch")
    others = peers(-1)
    barrier = meet(others)
    weights = [
        pltpu.make_async_copy(up_hbm.at[1], w_up, sems.at[0]),
        pltpu.make_async_copy(down_hbm.at[1], w_down, sems.at[1]),
    ]
    for copy in weights:
        copy.start()
    pl.semaphore_wait(barrier, SLOTS)
    pltpu.make_async_copy(send.at[0], arrived.at[0], recv_sem.at[0]).start()
    for slot in range(1, SLOTS):
        pltpu.make_async_remote_copy(
            send.at[slot], arrived.at[slot], send_sem, recv_sem.at[slot],
            device_id=(core, others[slot]), device_id_type=MESH,
        ).start()
    for copy in weights:
        copy.wait()

    def step(batch, carry):
        for index in range(BATCH):
            slot = batch * BATCH + index
            pltpu.make_async_copy(send.at[slot], arrived.at[slot], recv_sem.at[slot]).wait()
        batch_mlp(batch, arrived, done, gains[2:3, :], w_up, w_down)
        return carry

    lax.fori_loop(0, BATCHES, step, 0)
    remote = pl.ds(1, SLOTS - 1)
    pltpu.make_async_remote_copy(
        send.at[remote], arrived.at[remote], send_sem, recv_sem.at[0],
        device_id=(1 - core, lax.axis_index("cells")), device_id_type=MESH,
    ).wait_send()
    position = lax.broadcasted_iota(jnp.int32, (CELL, C), 0)
    for cell in range(CELLS_DEV):
        rows = done[slots[cell]].astype(jnp.float32)
        count = counts[cell // HALF_CELLS, cell % HALF_CELLS]
        out[cell] = jnp.where(position < count, rows, 0.0).astype(jnp.bfloat16)


def any_spec():
    return pl.BlockSpec(memory_space=pl.ANY)


def vmem_spec():
    return pl.BlockSpec(memory_space=pltpu.VMEM)


def smem_spec():
    return pl.BlockSpec(memory_space=pltpu.SMEM)


def shards(features, hilbert_rank, valid_count, norm_gains, w_qkv, w_out, w_up, w_down):
    slab = jax.ShapeDtypeStruct((SLOTS, CELL, C), jnp.bfloat16)
    label_shape = jax.ShapeDtypeStruct((SLOTS, 1, 128), jnp.int32)
    dma = pltpu.SemaphoreType.DMA
    slab_vmem = pltpu.VMEM((SLOTS, CELL, C), jnp.bfloat16)
    up_vmem = pltpu.VMEM((C, FF), jnp.bfloat16)
    down_vmem = pltpu.VMEM((FF, C), jnp.bfloat16)
    cell_of, labels, slots = pl.pallas_call(
        table_kernel,
        out_shape=(
            jax.ShapeDtypeStruct((SLOTS,), jnp.int32),
            label_shape,
            jax.ShapeDtypeStruct((CELLS_DEV,), jnp.int32),
        ),
        in_specs=[smem_spec(), smem_spec()],
        out_specs=(smem_spec(), vmem_spec(), smem_spec()),
        scratch_shapes=[
            pltpu.SMEM((SLOTS,), jnp.int32),
            pltpu.SMEM((SLOTS,), jnp.int32),
            pltpu.SMEM((SLOTS,), jnp.int32),
        ],
        name="tables",
    )(hilbert_rank, valid_count)

    own, other, own_labels, other_labels = pl.pallas_call(
        forward_kernel,
        out_shape=(slab, slab, label_shape, label_shape),
        in_specs=[smem_spec(), vmem_spec(), vmem_spec(), vmem_spec(), any_spec(), any_spec()],
        out_specs=(any_spec(), any_spec(), any_spec(), any_spec()),
        scratch_shapes=[
            slab_vmem, slab_vmem, pltpu.VMEM((SLOTS, 1, 128), jnp.int32), slab_vmem,
            up_vmem, down_vmem,
            dma, dma((SLOTS,)), dma, dma,
            dma((BATCHES,)), dma((BATCHES,)), dma((BATCHES,)), dma((4,)), dma((2,)),
        ],
        compiler_params=pltpu.CompilerParams(
            collective_id=0, has_side_effects=True, vmem_limit_bytes=VMEM_LIMIT
        ),
        name="forward",
    )(cell_of, labels, features.reshape(CELLS_DEV, CELL, C), norm_gains, w_up, w_down)

    send = pl.pallas_call(
        layer_kernel,
        out_shape=slab,
        in_specs=[smem_spec(), smem_spec(), vmem_spec(), vmem_spec(), vmem_spec()]
        + [any_spec()] * 2,
        out_specs=vmem_spec(),
        scratch_shapes=[
            pltpu.VMEM((2, PATCH_ROWS + 2 * TK, C), jnp.float32),
            pltpu.VMEM((GROUPS, PATCH_ROWS, GROUP_LANES), jnp.bfloat16),
            pltpu.VMEM((GROUPS, PATCH_ROWS, GROUP_LANES), jnp.bfloat16),
            pltpu.VMEM((GROUPS, GROUP_LANES + DEPTH, PATCH_ROWS), jnp.bfloat16),
            pltpu.VMEM((HALF_ROWS, C), jnp.bfloat16),
            pltpu.VMEM((2, PATCH_ROWS, STACK), jnp.float32),
            pltpu.VMEM((C, 3 * C), jnp.bfloat16),
            pltpu.VMEM((C, C), jnp.bfloat16),
            pltpu.SMEM((CELLS_DEV,), jnp.int32),
            pltpu.SMEM((SLOTS + 1,), jnp.int32),
            pltpu.SMEM((SLOTS + 1,), jnp.int32),
            dma((2,)),
        ],
        compiler_params=pltpu.CompilerParams(vmem_limit_bytes=VMEM_LIMIT),
        name="layer",
    )(
        own_labels.reshape(SLOTS, 128), other_labels.reshape(SLOTS, 128), own, other, norm_gains,
        w_qkv, w_out,
    )

    out = pl.pallas_call(
        return_kernel,
        out_shape=jax.ShapeDtypeStruct((CELLS_DEV, CELL, C), jnp.bfloat16),
        in_specs=[smem_spec(), smem_spec(), any_spec(), vmem_spec(), any_spec(), any_spec()],
        out_specs=vmem_spec(),
        scratch_shapes=[
            slab_vmem, slab_vmem, up_vmem, down_vmem, dma, dma((SLOTS,)), dma((2,)),
        ],
        compiler_params=pltpu.CompilerParams(
            collective_id=1, has_side_effects=True, vmem_limit_bytes=VMEM_LIMIT
        ),
        name="homeward",
    )(slots, valid_count, send, norm_gains, w_up, w_down)
    return out.reshape(features.shape)


def solution(mesh):
    in_specs = (
        P("cells", "patch", None),
        P("cells", "patch"),
        P("cells", "patch"),
        P(),
        P(),
        P(),
        P(),
        P(),
    )
    out_specs = P("cells", "patch", None)
    return jax.shard_map(shards, mesh=mesh, in_specs=in_specs, out_specs=out_specs, check_vma=False)
```

```python
import functools
import itertools
import math
import random

import jax
import jax.numpy as jnp
from jax import lax
from jax.experimental import pallas as pl
from jax.experimental.pallas import tpu as pltpu
from jax.sharding import PartitionSpec as P

MESH = pl.DeviceIdType.MESH
EPSILON = 1e-05
C = 512
FF = 2048
CELL = 32
SIDE = 4
SLOTS = SIDE**3
CELLS_DEV = 32
HALF_CELLS = 16
HALF_ROWS = 512
PATCH_ROWS = 1024
GROUPS = 4
GROUP_LANES = 128
GROUP_HEADS = 8
DEPTH = 16
GELU_LINEAR = math.sqrt(2 / math.pi)
GELU_CUBIC = 0.044715 * GELU_LINEAR
QUERY_SCALE = DEPTH**-0.5 * math.log2(math.e)
TM = 128
TQ = 32
TK = 128
STACK = GROUP_HEADS * TQ
FORWARD_LIMIT = 48 * 1024 * 1024
LAYER_LIMIT = 32 * 1024 * 1024
RETURN_LIMIT = 20 * 1024 * 1024

OFFSETS = [o for o in itertools.product(range(SIDE), repeat=3) if o != (0, 0, 0)]
random.Random(0).shuffle(OFFSETS)
OFFSETS = [(0, 0, 0)] + OFFSETS
BATCH = 4
BATCHES = SLOTS // BATCH


def number(offset):
    return (offset[0] * SIDE + offset[1]) * SIDE + offset[2]


def peers(sign):
    me = lax.axis_index("cells")
    ys = [lax.rem(lax.div(me, 16) + d, SIDE) * 16 for d in range(SIDE)]
    xs = [lax.rem(lax.div(me, 4) + d, SIDE) * 4 for d in range(SIDE)]
    zs = [lax.rem(me + d, SIDE) for d in range(SIDE)]
    return [
        ys[sign * oy % SIDE] + xs[sign * ox % SIDE] + zs[sign * oz % SIDE]
        for oy, ox, oz in OFFSETS
    ]


def norm_rows(values, gains):
    center = values - jnp.mean(values, axis=-1, keepdims=True)
    spread = jnp.mean(center * center, axis=-1, keepdims=True)
    return (center * lax.rsqrt(spread + EPSILON) * gains).astype(jnp.bfloat16)


def gelu(value):
    inner = value * (GELU_LINEAR + GELU_CUBIC * (value * value))
    half = 0.5 * value
    return (half + half * jnp.tanh(inner)).astype(jnp.bfloat16)


def mlp_rows(rows, gain_row, w_up, w_down):
    normed = norm_rows(rows, gain_row)
    raised = jnp.dot(normed, w_up[...], preferred_element_type=jnp.float32)
    return rows + jnp.dot(gelu(raised), w_down[...], preferred_element_type=jnp.float32)


def put_rows(ref, start, rows):
    base = pl.multiple_of((start >> 3) << 3, 8)
    shift = start - base
    padded = jnp.concatenate([rows, jnp.zeros((8, C), jnp.float32)], axis=0)
    moved = pltpu.roll(padded, shift, 0)
    position = lax.broadcasted_iota(jnp.int32, (8, C), 0)
    pltpu.store(ref.at[pl.ds(base, 8), :], moved[:8], mask=position >= shift)
    ref[pl.ds(pl.multiple_of(base + 8, 8), CELL), :] = moved[8:]


def take_rows(ref, start):
    base = pl.multiple_of((start >> 3) << 3, 8)
    window = ref[pl.ds(base, CELL + 8), :]
    ahead = start - base
    return pltpu.roll(window, jnp.where(ahead == 0, 0, CELL + 8 - ahead), 0)[:CELL]


def table_kernel(rank_ref, count_ref, cell_of, labels, slots, place, label_of, found):
    me = lax.axis_index("cells")
    y, x, z = me >> 4, (me >> 2) & 3, me & 3
    for slot, offset in enumerate(OFFSETS):
        place[number(offset)] = slot
        label_of[slot] = 0
        found[slot] = 0

    def one(cell, carry):
        rank = rank_ref[cell >> 4, cell & 15]
        owner = rank >> 6
        oy = ((owner >> 4) - y) & 3
        ox = (((owner >> 2) & 3) - x) & 3
        oz = ((owner & 3) - z) & 3
        slot = place[(oy << 4) | (ox << 2) | oz]
        slots[cell] = slot
        found[slot] = cell
        label_of[slot] = count_ref[cell >> 4, cell & 15] + 64 * ((rank >> 5) & 1)
        return carry

    lax.fori_loop(0, CELLS_DEV, one, 0)
    for slot in range(SLOTS):
        cell_of[slot] = found[slot]
        labels[slot] = jnp.full((1, 128), label_of[slot], jnp.int32)


def meet(others):
    core = lax.axis_index("patch")
    barrier = pltpu.get_barrier_semaphore()
    for other in others[1:]:
        pl.semaphore_signal(barrier, inc=1, device_id=(core, other), device_id_type=MESH)
    pl.semaphore_signal(
        barrier, inc=1, device_id=(1 - core, lax.axis_index("cells")), device_id_type=MESH
    )
    return barrier


def batch_mlp(batch, arrived, done, gain_row, w_up, w_down):
    slots = pl.ds(pl.multiple_of(batch * BATCH, BATCH), BATCH)
    rows = arrived[slots].reshape(BATCH * CELL, C).astype(jnp.float32)
    rows = mlp_rows(rows, gain_row, w_up, w_down)
    done[slots] = rows.astype(jnp.bfloat16).reshape(BATCH, CELL, C)


def forward_kernel(
    cell_of, labels, features, gains, up_hbm, down_hbm, own, other, own_labels, other_labels,
    send, arrived, arrived_labels, done, w_up, w_down,
    send_sem, recv_sem, label_send, label_recv, keep_sem, pass_sem, got_sem, tail_sem, sems,
):
    core = lax.axis_index("patch")
    sibling = (1 - core, lax.axis_index("cells"))
    others = peers(1)
    barrier = meet(others)
    weights = [
        pltpu.make_async_copy(up_hbm.at[0], w_up, sems.at[0]),
        pltpu.make_async_copy(down_hbm.at[0], w_down, sems.at[1]),
    ]
    for copy in weights:
        copy.start()
    for slot in range(SLOTS):
        send[slot] = features[cell_of[slot]]
    pl.semaphore_wait(barrier, SLOTS)

    pltpu.make_async_copy(send.at[0], arrived.at[0], recv_sem.at[0]).start()
    local_labels = pltpu.make_async_copy(labels.at[0], arrived_labels.at[0], tail_sem.at[3])
    local_labels.start()
    for slot in range(1, SLOTS):
        pltpu.make_async_remote_copy(
            send.at[slot], arrived.at[slot], send_sem, recv_sem.at[slot],
            device_id=(core, others[slot]), device_id_type=MESH,
        ).start()
    for slot in range(1, SLOTS):
        pltpu.make_async_remote_copy(
            labels.at[slot], arrived_labels.at[slot], label_send, label_recv,
            device_id=(core, others[slot]), device_id_type=MESH,
        ).start()
    for copy in weights:
        copy.wait()

    def step(batch, carry):
        for index in range(BATCH):
            slot = batch * BATCH + index
            pltpu.make_async_copy(send.at[slot], arrived.at[slot], recv_sem.at[slot]).wait()
        batch_mlp(batch, arrived, done, gains[0:1, :], w_up, w_down)
        slots = pl.ds(pl.multiple_of(batch * BATCH, BATCH), BATCH)
        pltpu.make_async_copy(done.at[slots], own.at[slots], keep_sem.at[batch]).start()
        pltpu.make_async_remote_copy(
            done.at[slots], other.at[slots], pass_sem.at[batch], got_sem.at[batch],
            device_id=sibling, device_id_type=MESH,
        ).start()
        return carry

    lax.fori_loop(0, BATCHES, step, 0)
    remote = pl.ds(1, SLOTS - 1)
    all_labels = pltpu.make_async_remote_copy(
        labels.at[remote], arrived_labels.at[remote], label_send, label_recv,
        device_id=sibling, device_id_type=MESH,
    )
    all_labels.wait_recv()
    local_labels.wait()
    keep_labels = pltpu.make_async_copy(arrived_labels, own_labels, tail_sem.at[0])
    pass_labels = pltpu.make_async_remote_copy(
        arrived_labels, other_labels, tail_sem.at[1], tail_sem.at[2],
        device_id=sibling, device_id_type=MESH,
    )
    keep_labels.start()
    pass_labels.start()
    all_labels.wait_send()
    pltpu.make_async_remote_copy(
        send.at[remote], arrived.at[remote], send_sem, recv_sem.at[0],
        device_id=sibling, device_id_type=MESH,
    ).wait_send()

    def drain(batch, carry):
        slots = pl.ds(pl.multiple_of(batch * BATCH, BATCH), BATCH)
        pltpu.make_async_copy(done.at[slots], own.at[slots], keep_sem.at[batch]).wait()
        pltpu.make_async_remote_copy(
            done.at[slots], other.at[slots], pass_sem.at[batch], got_sem.at[batch],
            device_id=sibling, device_id_type=MESH,
        ).wait()
        return carry

    lax.fori_loop(0, BATCHES, drain, 0)
    keep_labels.wait()
    pass_labels.wait()


def layer_kernel(
    own_labels, other_labels, own, other, gains, w_qkv, w_out,
    send, packed, queries, keys, values, mixed, ahead, offsets, own_filled, other_filled,
):
    def pack(labels, cells, filled, starts):
        count = jnp.int32(0)
        for slot in range(SLOTS):
            filled[count] = slot
            count = count + jnp.where(labels[slot, 0] > 0, 1, 0)

        def one(cell, starts):
            slot = filled[cell]
            label = labels[slot, 0]
            patch = label >> 6
            count = label & 63
            start = jnp.where(patch == 0, starts[0], starts[1])
            if labels is own_labels:
                offsets[cell] = start
            put_rows(packed.at[patch], start, cells[slot].astype(jnp.float32))
            first = jnp.where(patch == 0, count, 0)
            return starts[0] + first, starts[1] + count - first

        return lax.fori_loop(0, CELLS_DEV, one, starts, unroll=4)

    pack_own = functools.partial(pack, own_labels, own, own_filled)
    pack_other = functools.partial(pack, other_labels, other, other_filled)
    query_rows = pack_own((jnp.int32(0), jnp.int32(0)))
    key_rows = pack_other(query_rows)
    lane = lax.broadcasted_iota(jnp.int32, (1, GROUP_LANES), 1) // DEPTH
    head_masks = [(lane == head).astype(jnp.float32) for head in range(GROUP_HEADS)]

    def project(patch, key_count, step, carry):
        base = pl.multiple_of(step * TM, TM)
        rows = pl.ds(base, TM)
        normed = norm_rows(packed[patch, rows, :], gains[1:2, :])
        raw = jnp.dot(normed, w_qkv[...], preferred_element_type=jnp.float32)
        projected = raw.astype(jnp.bfloat16)
        seen = lax.broadcasted_iota(jnp.int32, (GROUP_LANES, TM), 1) + base < key_count
        ones = lax.broadcasted_iota(jnp.int32, (DEPTH, TM), 1) + base < key_count
        for group in range(GROUPS):
            low = group * GROUP_LANES
            query = raw[:, low : low + GROUP_LANES] * QUERY_SCALE
            queries[group, rows, :] = query.astype(jnp.bfloat16)
            keys[group, rows, :] = projected[:, C + low : C + low + GROUP_LANES]
            value = projected[:, 2 * C + low : 2 * C + low + GROUP_LANES].astype(jnp.float32)
            values[group, :GROUP_LANES, rows] = jnp.where(seen, value.T, 0.0).astype(jnp.bfloat16)
            values[group, GROUP_LANES:, rows] = jnp.where(ones, 1.0, 0.0).astype(jnp.bfloat16)
        return carry

    fold = lax.broadcasted_iota(jnp.int32, (TQ, STACK), 1) % TQ
    fold = fold == lax.broadcasted_iota(jnp.int32, (TQ, STACK), 0)
    fold = fold.astype(jnp.float32).astype(jnp.bfloat16)
    block = lax.broadcasted_iota(jnp.int32, (GROUP_LANES, STACK), 0) // DEPTH
    block = block == lax.broadcasted_iota(jnp.int32, (GROUP_LANES, STACK), 1) // TQ

    def score(group, key_span, tile):
        query = queries[group, pl.ds(pl.multiple_of(tile * TQ, TQ), TQ), :].astype(jnp.float32)
        stacked = jnp.concatenate([query * mask for mask in head_masks], axis=0)
        return lax.dot_general(
            keys[group, :key_span, :], stacked.astype(jnp.bfloat16),
            (((1,), (1,)), ((), ())), preferred_element_type=jnp.float32,
        )

    def weigh(scores):
        highest = jnp.max(scores, axis=0, keepdims=True)
        return jnp.exp2(scores - highest).astype(jnp.bfloat16)

    def mix(group, key_span, weights):
        mixture = jnp.dot(
            values[group, :, :key_span], weights, preferred_element_type=jnp.float32
        )
        top = mixture[:GROUP_LANES] / mixture[GROUP_LANES : GROUP_LANES + 1]
        return jnp.where(block, top, 0.0).astype(jnp.bfloat16)

    def attend(key_span, steps):
        ahead[0, :key_span, :] = score(0, key_span, 0)
        ahead[1, :key_span, :] = score(1, key_span, 0)

        def one(step, carry):
            rows = pl.ds(pl.multiple_of(step * TQ, TQ), TQ)
            following = jnp.minimum(step + 1, steps - 1)
            late = [score(2, key_span, step), score(3, key_span, step)]
            weights = [weigh(ahead[0, :key_span, :]), weigh(ahead[1, :key_span, :])]
            tops = [mix(group, key_span, weights[group]) for group in range(2)]
            early = [score(0, key_span, following), score(1, key_span, following)]
            weights = [weigh(value) for value in late]
            for group in range(2):
                ahead[group, :key_span, :] = early[group]
            tops += [mix(group + 2, key_span, weights[group]) for group in range(2)]
            for group, top in enumerate(tops):
                low = group * GROUP_LANES
                mixed[rows, low : low + GROUP_LANES] = lax.dot_general(
                    fold, top, (((1,), (1,)), ((), ())), preferred_element_type=jnp.float32
                ).astype(jnp.bfloat16)
            return carry

        lax.fori_loop(0, steps, one, 0)

    def finish(patch, step, carry):
        rows = pl.ds(pl.multiple_of(step * TM, TM), TM)
        middle = packed[patch, rows, :] + jnp.dot(
            mixed[rows, :], w_out[...], preferred_element_type=jnp.float32
        )
        packed[patch, rows, :] = middle
        return carry

    def one_patch(patch, carry):
        query_count = jnp.where(patch == 0, query_rows[0], query_rows[1])
        key_count = jnp.where(patch == 0, key_rows[0], key_rows[1])
        base = pl.multiple_of(key_count // 8 * 8, 8)
        spare = jnp.broadcast_to(packed[patch, 0:1, :], (8, C))
        edge = packed[patch, pl.ds(base, 8), :]
        position = lax.broadcasted_iota(jnp.int32, (8, C), 0)
        packed[patch, pl.ds(base, 8), :] = jnp.where(position < key_count - base, edge, spare)
        packed[patch, pl.ds(pl.multiple_of(base + 8, 8), TK), :] = jnp.broadcast_to(spare[:1], (TK, C))
        key_tiles = (key_count + TK - 1) // TK
        lax.fori_loop(0, key_tiles, functools.partial(project, patch, key_count), 0)
        steps = (query_count + TQ - 1) // TQ
        for tiles in range(1, PATCH_ROWS // TK + 1):

            @pl.when(key_tiles == tiles)
            def _():
                attend(tiles * TK, steps)

        lax.fori_loop(0, (query_count + TM - 1) // TM, functools.partial(finish, patch), 0)
        return carry

    lax.fori_loop(0, 2, one_patch, 0)

    def unpack(cell, carry):
        slot = own_filled[cell]
        rows = take_rows(packed.at[own_labels[slot, 0] >> 6], offsets[cell])
        send[slot] = rows.astype(jnp.bfloat16)
        return carry

    lax.fori_loop(0, CELLS_DEV, unpack, 0, unroll=4)


def return_kernel(
    slots, counts, send, gains, up_hbm, down_hbm, out,
    arrived, done, w_up, w_down, send_sem, recv_sem, sems,
):
    core = lax.axis_index("patch")
    others = peers(-1)
    barrier = meet(others)
    weights = [
        pltpu.make_async_copy(up_hbm.at[1], w_up, sems.at[0]),
        pltpu.make_async_copy(down_hbm.at[1], w_down, sems.at[1]),
    ]
    for copy in weights:
        copy.start()
    pl.semaphore_wait(barrier, SLOTS)
    pltpu.make_async_copy(send.at[0], arrived.at[0], recv_sem.at[0]).start()
    for slot in range(1, SLOTS):
        pltpu.make_async_remote_copy(
            send.at[slot], arrived.at[slot], send_sem, recv_sem.at[slot],
            device_id=(core, others[slot]), device_id_type=MESH,
        ).start()
    for copy in weights:
        copy.wait()

    def step(batch, carry):
        for index in range(BATCH):
            slot = batch * BATCH + index
            pltpu.make_async_copy(send.at[slot], arrived.at[slot], recv_sem.at[slot]).wait()
        batch_mlp(batch, arrived, done, gains[2:3, :], w_up, w_down)
        return carry

    lax.fori_loop(0, BATCHES, step, 0)
    remote = pl.ds(1, SLOTS - 1)
    pltpu.make_async_remote_copy(
        send.at[remote], arrived.at[remote], send_sem, recv_sem.at[0],
        device_id=(1 - core, lax.axis_index("cells")), device_id_type=MESH,
    ).wait_send()
    position = lax.broadcasted_iota(jnp.int32, (CELL, C), 0)
    for cell in range(CELLS_DEV):
        rows = done[slots[cell]].astype(jnp.float32)
        count = counts[cell // HALF_CELLS, cell % HALF_CELLS]
        out[cell] = jnp.where(position < count, rows, 0.0).astype(jnp.bfloat16)


def any_spec():
    return pl.BlockSpec(memory_space=pl.ANY)


def hbm_spec():
    return pl.BlockSpec(memory_space=pltpu.HBM)


def vmem_spec():
    return pl.BlockSpec(memory_space=pltpu.VMEM)


def smem_spec():
    return pl.BlockSpec(memory_space=pltpu.SMEM)


def shards(features, hilbert_rank, valid_count, norm_gains, w_qkv, w_out, w_up, w_down):
    slab = jax.ShapeDtypeStruct((SLOTS, CELL, C), jnp.bfloat16)
    label_shape = jax.ShapeDtypeStruct((SLOTS, 1, 128), jnp.int32)
    dma = pltpu.SemaphoreType.DMA
    slab_vmem = pltpu.VMEM((SLOTS, CELL, C), jnp.bfloat16)
    up_vmem = pltpu.VMEM((C, FF), jnp.bfloat16)
    down_vmem = pltpu.VMEM((FF, C), jnp.bfloat16)
    cell_of, labels, slots = pl.pallas_call(
        table_kernel,
        out_shape=(
            jax.ShapeDtypeStruct((SLOTS,), jnp.int32),
            label_shape,
            jax.ShapeDtypeStruct((CELLS_DEV,), jnp.int32),
        ),
        in_specs=[smem_spec(), smem_spec()],
        out_specs=(smem_spec(), vmem_spec(), smem_spec()),
        scratch_shapes=[
            pltpu.SMEM((SLOTS,), jnp.int32),
            pltpu.SMEM((SLOTS,), jnp.int32),
            pltpu.SMEM((SLOTS,), jnp.int32),
        ],
        compiler_params=pltpu.CompilerParams(vmem_limit_bytes=4 * 1024 * 1024),
        cost_estimate=pl.CostEstimate(flops=10**9, bytes_accessed=4 * 10**6, transcendentals=0),
        name="tables",
    )(hilbert_rank, valid_count)

    own, other, own_labels, other_labels = pl.pallas_call(
        forward_kernel,
        out_shape=(slab, slab, label_shape, label_shape),
        in_specs=[smem_spec(), vmem_spec(), vmem_spec(), vmem_spec(), hbm_spec(), hbm_spec()],
        out_specs=(any_spec(), any_spec(), any_spec(), any_spec()),
        scratch_shapes=[
            slab_vmem, slab_vmem, pltpu.VMEM((SLOTS, 1, 128), jnp.int32), slab_vmem,
            up_vmem, down_vmem,
            dma, dma((SLOTS,)), dma, dma,
            dma((BATCHES,)), dma((BATCHES,)), dma((BATCHES,)), dma((4,)), dma((2,)),
        ],
        compiler_params=pltpu.CompilerParams(
            collective_id=0, has_side_effects=True, vmem_limit_bytes=FORWARD_LIMIT
        ),
        cost_estimate=pl.CostEstimate(
            flops=2 * 10**10, bytes_accessed=4 * 10**7, transcendentals=0
        ),
        name="forward",
    )(cell_of, labels, features.reshape(CELLS_DEV, CELL, C), norm_gains, w_up, w_down)

    send = pl.pallas_call(
        layer_kernel,
        out_shape=slab,
        in_specs=[smem_spec(), smem_spec()] + [vmem_spec()] * 5,
        out_specs=vmem_spec(),
        scratch_shapes=[
            pltpu.VMEM((2, PATCH_ROWS + 2 * TK, C), jnp.float32),
            pltpu.VMEM((GROUPS, PATCH_ROWS, GROUP_LANES), jnp.bfloat16),
            pltpu.VMEM((GROUPS, PATCH_ROWS, GROUP_LANES), jnp.bfloat16),
            pltpu.VMEM((GROUPS, GROUP_LANES + DEPTH, PATCH_ROWS), jnp.bfloat16),
            pltpu.VMEM((HALF_ROWS, C), jnp.bfloat16),
            pltpu.VMEM((2, PATCH_ROWS, STACK), jnp.float32),
            pltpu.SMEM((CELLS_DEV,), jnp.int32),
            pltpu.SMEM((SLOTS + 1,), jnp.int32),
            pltpu.SMEM((SLOTS + 1,), jnp.int32),
        ],
        compiler_params=pltpu.CompilerParams(vmem_limit_bytes=LAYER_LIMIT),
        cost_estimate=pl.CostEstimate(
            flops=2 * 10**10, bytes_accessed=4 * 10**7, transcendentals=0
        ),
        name="layer",
    )(
        own_labels.reshape(SLOTS, 128), other_labels.reshape(SLOTS, 128), own, other, norm_gains,
        w_qkv, w_out,
    )

    out = pl.pallas_call(
        return_kernel,
        out_shape=jax.ShapeDtypeStruct((CELLS_DEV, CELL, C), jnp.bfloat16),
        in_specs=[smem_spec(), smem_spec(), any_spec(), vmem_spec(), hbm_spec(), hbm_spec()],
        out_specs=vmem_spec(),
        scratch_shapes=[
            slab_vmem, slab_vmem, up_vmem, down_vmem, dma, dma((SLOTS,)), dma((2,)),
        ],
        compiler_params=pltpu.CompilerParams(
            collective_id=1, has_side_effects=True, vmem_limit_bytes=RETURN_LIMIT
        ),
        cost_estimate=pl.CostEstimate(
            flops=2 * 10**10, bytes_accessed=4 * 10**7, transcendentals=0
        ),
        name="homeward",
    )(slots, valid_count, send, norm_gains, w_up, w_down)
    return out.reshape(features.shape)


def solution(mesh):
    in_specs = (
        P("cells", "patch", None),
        P("cells", "patch"),
        P("cells", "patch"),
        P(),
        P(),
        P(),
        P(),
        P(),
    )
    out_specs = P("cells", "patch", None)
    return jax.shard_map(shards, mesh=mesh, in_specs=in_specs, out_specs=out_specs, check_vma=False)
```

```python
import functools
import itertools
import math
import random

import jax
import jax.numpy as jnp
from jax import lax
from jax.experimental import pallas as pl
from jax.experimental.pallas import tpu as pltpu
from jax.sharding import PartitionSpec as P

MESH = pl.DeviceIdType.MESH
EPSILON = 1e-05
C = 512
FF = 2048
CELL = 32
SIDE = 4
SLOTS = SIDE**3
CELLS_DEV = 32
HALF_CELLS = 16
HALF_ROWS = 512
PATCH_ROWS = 1024
GROUPS = 4
GROUP_LANES = 128
GROUP_HEADS = 8
DEPTH = 16
GELU_LINEAR = math.sqrt(2 / math.pi)
GELU_CUBIC = 0.044715 * GELU_LINEAR
QUERY_SCALE = DEPTH**-0.5 * math.log2(math.e)
TM = 128
TQ = 32
TK = 128
STACK = GROUP_HEADS * TQ
FORWARD_LIMIT = 48 * 1024 * 1024
LAYER_LIMIT = 32 * 1024 * 1024
RETURN_LIMIT = 20 * 1024 * 1024

OFFSETS = [o for o in itertools.product(range(SIDE), repeat=3) if o != (0, 0, 0)]
random.Random(0).shuffle(OFFSETS)
OFFSETS = [(0, 0, 0)] + OFFSETS
BATCH = 4
BATCHES = SLOTS // BATCH


def number(offset):
    return (offset[0] * SIDE + offset[1]) * SIDE + offset[2]


def peers(sign):
    me = lax.axis_index("cells")
    ys = [lax.rem(lax.div(me, 16) + d, SIDE) * 16 for d in range(SIDE)]
    xs = [lax.rem(lax.div(me, 4) + d, SIDE) * 4 for d in range(SIDE)]
    zs = [lax.rem(me + d, SIDE) for d in range(SIDE)]
    return [
        ys[sign * oy % SIDE] + xs[sign * ox % SIDE] + zs[sign * oz % SIDE]
        for oy, ox, oz in OFFSETS
    ]


def norm_rows(values, gains):
    center = values - jnp.mean(values, axis=-1, keepdims=True)
    spread = jnp.mean(center * center, axis=-1, keepdims=True)
    return (center * lax.rsqrt(spread + EPSILON) * gains).astype(jnp.bfloat16)


def gelu(value):
    inner = value * (GELU_LINEAR + GELU_CUBIC * (value * value))
    half = 0.5 * value
    return (half + half * jnp.tanh(inner)).astype(jnp.bfloat16)


def mlp_rows(rows, gain_row, w_up, w_down):
    normed = norm_rows(rows, gain_row)
    raised = jnp.dot(normed, w_up[...], preferred_element_type=jnp.float32)
    return rows + jnp.dot(gelu(raised), w_down[...], preferred_element_type=jnp.float32)


def put_rows(ref, start, rows):
    base = pl.multiple_of((start >> 3) << 3, 8)
    shift = start - base
    padded = jnp.concatenate([rows, jnp.zeros((8, C), jnp.float32)], axis=0)
    moved = pltpu.roll(padded, shift, 0)
    position = lax.broadcasted_iota(jnp.int32, (8, C), 0)
    pltpu.store(ref.at[pl.ds(base, 8), :], moved[:8], mask=position >= shift)
    ref[pl.ds(pl.multiple_of(base + 8, 8), CELL), :] = moved[8:]


def take_rows(ref, start):
    base = pl.multiple_of((start >> 3) << 3, 8)
    window = ref[pl.ds(base, CELL + 8), :]
    ahead = start - base
    return pltpu.roll(window, jnp.where(ahead == 0, 0, CELL + 8 - ahead), 0)[:CELL]


def table_kernel(rank_ref, count_ref, cell_of, labels, slots, place, label_of, found):
    me = lax.axis_index("cells")
    y, x, z = me >> 4, (me >> 2) & 3, me & 3
    for slot, offset in enumerate(OFFSETS):
        place[number(offset)] = slot
        label_of[slot] = 0
        found[slot] = 0

    def one(cell, carry):
        rank = rank_ref[cell >> 4, cell & 15]
        owner = rank >> 6
        oy = ((owner >> 4) - y) & 3
        ox = (((owner >> 2) & 3) - x) & 3
        oz = ((owner & 3) - z) & 3
        slot = place[(oy << 4) | (ox << 2) | oz]
        slots[cell] = slot
        found[slot] = cell
        label_of[slot] = count_ref[cell >> 4, cell & 15] + 64 * ((rank >> 5) & 1)
        return carry

    lax.fori_loop(0, CELLS_DEV, one, 0)
    for slot in range(SLOTS):
        cell_of[slot] = found[slot]
        labels[slot] = jnp.full((1, 128), label_of[slot], jnp.int32)


def meet(others):
    core = lax.axis_index("patch")
    barrier = pltpu.get_barrier_semaphore()
    for other in others[1:]:
        pl.semaphore_signal(barrier, inc=1, device_id=(core, other), device_id_type=MESH)
    pl.semaphore_signal(
        barrier, inc=1, device_id=(1 - core, lax.axis_index("cells")), device_id_type=MESH
    )
    return barrier


def batch_mlp(batch, arrived, done, gain_row, w_up, w_down):
    slots = pl.ds(pl.multiple_of(batch * BATCH, BATCH), BATCH)
    rows = arrived[slots].reshape(BATCH * CELL, C).astype(jnp.float32)
    rows = mlp_rows(rows, gain_row, w_up, w_down)
    done[slots] = rows.astype(jnp.bfloat16).reshape(BATCH, CELL, C)


def forward_kernel(
    cell_of, labels, features, gains, up_hbm, down_hbm, own, other, own_labels, other_labels,
    send, arrived, arrived_labels, done, w_up, w_down,
    send_sem, recv_sem, label_send, label_recv, keep_sem, pass_sem, got_sem, tail_sem, sems,
):
    core = lax.axis_index("patch")
    sibling = (1 - core, lax.axis_index("cells"))
    others = peers(1)
    barrier = meet(others)
    weights = [
        pltpu.make_async_copy(up_hbm.at[0], w_up, sems.at[0]),
        pltpu.make_async_copy(down_hbm.at[0], w_down, sems.at[1]),
    ]
    for copy in weights:
        copy.start()
    for slot in range(SLOTS):
        send[slot] = features[cell_of[slot]]
    pl.semaphore_wait(barrier, SLOTS)

    pltpu.make_async_copy(send.at[0], arrived.at[0], recv_sem.at[0]).start()
    local_labels = pltpu.make_async_copy(labels.at[0], arrived_labels.at[0], tail_sem.at[3])
    local_labels.start()
    for slot in range(1, SLOTS):
        pltpu.make_async_remote_copy(
            send.at[slot], arrived.at[slot], send_sem, recv_sem.at[slot],
            device_id=(core, others[slot]), device_id_type=MESH,
        ).start()
    for slot in range(1, SLOTS):
        pltpu.make_async_remote_copy(
            labels.at[slot], arrived_labels.at[slot], label_send, label_recv,
            device_id=(core, others[slot]), device_id_type=MESH,
        ).start()
    for copy in weights:
        copy.wait()

    def step(batch, carry):
        for index in range(BATCH):
            slot = batch * BATCH + index
            pltpu.make_async_copy(send.at[slot], arrived.at[slot], recv_sem.at[slot]).wait()
        batch_mlp(batch, arrived, done, gains[0:1, :], w_up, w_down)
        slots = pl.ds(pl.multiple_of(batch * BATCH, BATCH), BATCH)
        pltpu.make_async_copy(done.at[slots], own.at[slots], keep_sem.at[batch]).start()
        pltpu.make_async_remote_copy(
            done.at[slots], other.at[slots], pass_sem.at[batch], got_sem.at[batch],
            device_id=sibling, device_id_type=MESH,
        ).start()
        return carry

    lax.fori_loop(0, BATCHES, step, 0)
    remote = pl.ds(1, SLOTS - 1)
    all_labels = pltpu.make_async_remote_copy(
        labels.at[remote], arrived_labels.at[remote], label_send, label_recv,
        device_id=sibling, device_id_type=MESH,
    )
    all_labels.wait_recv()
    local_labels.wait()
    keep_labels = pltpu.make_async_copy(arrived_labels, own_labels, tail_sem.at[0])
    pass_labels = pltpu.make_async_remote_copy(
        arrived_labels, other_labels, tail_sem.at[1], tail_sem.at[2],
        device_id=sibling, device_id_type=MESH,
    )
    keep_labels.start()
    pass_labels.start()
    all_labels.wait_send()
    pltpu.make_async_remote_copy(
        send.at[remote], arrived.at[remote], send_sem, recv_sem.at[0],
        device_id=sibling, device_id_type=MESH,
    ).wait_send()

    def drain(batch, carry):
        slots = pl.ds(pl.multiple_of(batch * BATCH, BATCH), BATCH)
        pltpu.make_async_copy(done.at[slots], own.at[slots], keep_sem.at[batch]).wait()
        pltpu.make_async_remote_copy(
            done.at[slots], other.at[slots], pass_sem.at[batch], got_sem.at[batch],
            device_id=sibling, device_id_type=MESH,
        ).wait()
        return carry

    lax.fori_loop(0, BATCHES, drain, 0)
    keep_labels.wait()
    pass_labels.wait()


def layer_kernel(
    own_labels, other_labels, own, other, gains, w_qkv, w_out,
    send, packed, queries, keys, values, mixed, ahead, behind, offsets, own_filled, other_filled,
):
    def pack(labels, cells, filled, starts):
        count = jnp.int32(0)
        for slot in range(SLOTS):
            filled[count] = slot
            count = count + jnp.where(labels[slot, 0] > 0, 1, 0)

        def one(cell, starts):
            slot = filled[cell]
            label = labels[slot, 0]
            patch = label >> 6
            count = label & 63
            start = jnp.where(patch == 0, starts[0], starts[1])
            if labels is own_labels:
                offsets[cell] = start
            put_rows(packed.at[patch], start, cells[slot].astype(jnp.float32))
            first = jnp.where(patch == 0, count, 0)
            return starts[0] + first, starts[1] + count - first

        return lax.fori_loop(0, CELLS_DEV, one, starts, unroll=4)

    pack_own = functools.partial(pack, own_labels, own, own_filled)
    pack_other = functools.partial(pack, other_labels, other, other_filled)
    query_rows = pack_own((jnp.int32(0), jnp.int32(0)))
    key_rows = pack_other(query_rows)
    lane = lax.broadcasted_iota(jnp.int32, (1, GROUP_LANES), 1) // DEPTH
    head_masks = [(lane == head).astype(jnp.float32) for head in range(GROUP_HEADS)]

    def project(patch, key_count, step, carry):
        base = pl.multiple_of(step * TM, TM)
        rows = pl.ds(base, TM)
        normed = norm_rows(packed[patch, rows, :], gains[1:2, :])
        raw = jnp.dot(normed, w_qkv[...], preferred_element_type=jnp.float32)
        projected = raw.astype(jnp.bfloat16)
        seen = lax.broadcasted_iota(jnp.int32, (GROUP_LANES, TM), 1) + base < key_count
        ones = lax.broadcasted_iota(jnp.int32, (DEPTH, TM), 1) + base < key_count
        for group in range(GROUPS):
            low = group * GROUP_LANES
            query = raw[:, low : low + GROUP_LANES] * QUERY_SCALE
            queries[group, rows, :] = query.astype(jnp.bfloat16)
            keys[group, rows, :] = projected[:, C + low : C + low + GROUP_LANES]
            value = projected[:, 2 * C + low : 2 * C + low + GROUP_LANES].astype(jnp.float32)
            values[group, :GROUP_LANES, rows] = jnp.where(seen, value.T, 0.0).astype(jnp.bfloat16)
            values[group, GROUP_LANES:, rows] = jnp.where(ones, 1.0, 0.0).astype(jnp.bfloat16)
        return carry

    fold = lax.broadcasted_iota(jnp.int32, (TQ, STACK), 1) % TQ
    fold = fold == lax.broadcasted_iota(jnp.int32, (TQ, STACK), 0)
    fold = fold.astype(jnp.float32).astype(jnp.bfloat16)
    block = lax.broadcasted_iota(jnp.int32, (GROUP_LANES, STACK), 0) // DEPTH
    block = block == lax.broadcasted_iota(jnp.int32, (GROUP_LANES, STACK), 1) // TQ

    def score(group, key_span, tile):
        query = queries[group, pl.ds(pl.multiple_of(tile * TQ, TQ), TQ), :].astype(jnp.float32)
        stacked = jnp.concatenate([query * mask for mask in head_masks], axis=0)
        return lax.dot_general(
            keys[group, :key_span, :], stacked.astype(jnp.bfloat16),
            (((1,), (1,)), ((), ())), preferred_element_type=jnp.float32,
        )

    def weigh(scores):
        highest = jnp.max(scores, axis=0, keepdims=True)
        return jnp.exp2(scores - highest).astype(jnp.bfloat16)

    def mix(group, key_span, weights):
        mixture = jnp.dot(
            values[group, :, :key_span], weights, preferred_element_type=jnp.float32
        )
        top = mixture[:GROUP_LANES] / mixture[GROUP_LANES : GROUP_LANES + 1]
        return jnp.where(block, top, 0.0).astype(jnp.bfloat16)

    def attend(key_span, steps):
        ahead[0, :key_span, :] = score(0, key_span, 0)
        ahead[1, :key_span, :] = score(1, key_span, 0)

        def one(step, carry):
            rows = pl.ds(pl.multiple_of(step * TQ, TQ), TQ)
            following = jnp.minimum(step + 1, steps - 1)
            late = [score(2, key_span, step), score(3, key_span, step)]
            weights = [weigh(ahead[0, :key_span, :]), weigh(ahead[1, :key_span, :])]
            for group in range(2):
                behind[group, :key_span, :] = late[group]
            early = [score(0, key_span, following), score(1, key_span, following)]
            tops = [mix(group, key_span, weights[group]) for group in range(2)]
            weights = [weigh(behind[group, :key_span, :]) for group in range(2)]
            for group in range(2):
                ahead[group, :key_span, :] = early[group]
            tops += [mix(group + 2, key_span, weights[group]) for group in range(2)]
            for group, top in enumerate(tops):
                low = group * GROUP_LANES
                mixed[rows, low : low + GROUP_LANES] = lax.dot_general(
                    fold, top, (((1,), (1,)), ((), ())), preferred_element_type=jnp.float32
                ).astype(jnp.bfloat16)
            return carry

        lax.fori_loop(0, steps, one, 0)

    def finish(patch, step, carry):
        rows = pl.ds(pl.multiple_of(step * TM, TM), TM)
        middle = packed[patch, rows, :] + jnp.dot(
            mixed[rows, :], w_out[...], preferred_element_type=jnp.float32
        )
        packed[patch, rows, :] = middle
        return carry

    def one_patch(patch, carry):
        query_count = jnp.where(patch == 0, query_rows[0], query_rows[1])
        key_count = jnp.where(patch == 0, key_rows[0], key_rows[1])
        base = pl.multiple_of(key_count // 8 * 8, 8)
        spare = jnp.broadcast_to(packed[patch, 0:1, :], (8, C))
        edge = packed[patch, pl.ds(base, 8), :]
        position = lax.broadcasted_iota(jnp.int32, (8, C), 0)
        packed[patch, pl.ds(base, 8), :] = jnp.where(position < key_count - base, edge, spare)
        packed[patch, pl.ds(pl.multiple_of(base + 8, 8), TK), :] = jnp.broadcast_to(spare[:1], (TK, C))
        key_tiles = (key_count + TK - 1) // TK
        lax.fori_loop(0, key_tiles, functools.partial(project, patch, key_count), 0)
        steps = (query_count + TQ - 1) // TQ
        for tiles in range(1, PATCH_ROWS // TK + 1):

            @pl.when(key_tiles == tiles)
            def _():
                attend(tiles * TK, steps)

        lax.fori_loop(0, (query_count + TM - 1) // TM, functools.partial(finish, patch), 0)
        return carry

    lax.fori_loop(0, 2, one_patch, 0)

    def unpack(cell, carry):
        slot = own_filled[cell]
        rows = take_rows(packed.at[own_labels[slot, 0] >> 6], offsets[cell])
        send[slot] = rows.astype(jnp.bfloat16)
        return carry

    lax.fori_loop(0, CELLS_DEV, unpack, 0, unroll=4)


def return_kernel(
    slots, counts, send, gains, up_hbm, down_hbm, out,
    arrived, done, w_up, w_down, send_sem, recv_sem, sems,
):
    core = lax.axis_index("patch")
    others = peers(-1)
    barrier = meet(others)
    weights = [
        pltpu.make_async_copy(up_hbm.at[1], w_up, sems.at[0]),
        pltpu.make_async_copy(down_hbm.at[1], w_down, sems.at[1]),
    ]
    for copy in weights:
        copy.start()
    pl.semaphore_wait(barrier, SLOTS)
    pltpu.make_async_copy(send.at[0], arrived.at[0], recv_sem.at[0]).start()
    for slot in range(1, SLOTS):
        pltpu.make_async_remote_copy(
            send.at[slot], arrived.at[slot], send_sem, recv_sem.at[slot],
            device_id=(core, others[slot]), device_id_type=MESH,
        ).start()
    for copy in weights:
        copy.wait()

    def step(batch, carry):
        for index in range(BATCH):
            slot = batch * BATCH + index
            pltpu.make_async_copy(send.at[slot], arrived.at[slot], recv_sem.at[slot]).wait()
        batch_mlp(batch, arrived, done, gains[2:3, :], w_up, w_down)
        return carry

    lax.fori_loop(0, BATCHES, step, 0)
    remote = pl.ds(1, SLOTS - 1)
    pltpu.make_async_remote_copy(
        send.at[remote], arrived.at[remote], send_sem, recv_sem.at[0],
        device_id=(1 - core, lax.axis_index("cells")), device_id_type=MESH,
    ).wait_send()
    position = lax.broadcasted_iota(jnp.int32, (CELL, C), 0)
    for cell in range(CELLS_DEV):
        rows = done[slots[cell]].astype(jnp.float32)
        count = counts[cell // HALF_CELLS, cell % HALF_CELLS]
        out[cell] = jnp.where(position < count, rows, 0.0).astype(jnp.bfloat16)


def any_spec():
    return pl.BlockSpec(memory_space=pl.ANY)


def hbm_spec():
    return pl.BlockSpec(memory_space=pltpu.HBM)


def vmem_spec():
    return pl.BlockSpec(memory_space=pltpu.VMEM)


def smem_spec():
    return pl.BlockSpec(memory_space=pltpu.SMEM)


def shards(features, hilbert_rank, valid_count, norm_gains, w_qkv, w_out, w_up, w_down):
    slab = jax.ShapeDtypeStruct((SLOTS, CELL, C), jnp.bfloat16)
    label_shape = jax.ShapeDtypeStruct((SLOTS, 1, 128), jnp.int32)
    dma = pltpu.SemaphoreType.DMA
    slab_vmem = pltpu.VMEM((SLOTS, CELL, C), jnp.bfloat16)
    up_vmem = pltpu.VMEM((C, FF), jnp.bfloat16)
    down_vmem = pltpu.VMEM((FF, C), jnp.bfloat16)
    cell_of, labels, slots = pl.pallas_call(
        table_kernel,
        out_shape=(
            jax.ShapeDtypeStruct((SLOTS,), jnp.int32),
            label_shape,
            jax.ShapeDtypeStruct((CELLS_DEV,), jnp.int32),
        ),
        in_specs=[smem_spec(), smem_spec()],
        out_specs=(smem_spec(), vmem_spec(), smem_spec()),
        scratch_shapes=[
            pltpu.SMEM((SLOTS,), jnp.int32),
            pltpu.SMEM((SLOTS,), jnp.int32),
            pltpu.SMEM((SLOTS,), jnp.int32),
        ],
        compiler_params=pltpu.CompilerParams(vmem_limit_bytes=4 * 1024 * 1024),
        cost_estimate=pl.CostEstimate(flops=10**9, bytes_accessed=4 * 10**6, transcendentals=0),
        name="tables",
    )(hilbert_rank, valid_count)

    own, other, own_labels, other_labels = pl.pallas_call(
        forward_kernel,
        out_shape=(slab, slab, label_shape, label_shape),
        in_specs=[smem_spec(), vmem_spec(), vmem_spec(), vmem_spec(), hbm_spec(), hbm_spec()],
        out_specs=(any_spec(), any_spec(), any_spec(), any_spec()),
        scratch_shapes=[
            slab_vmem, slab_vmem, pltpu.VMEM((SLOTS, 1, 128), jnp.int32), slab_vmem,
            up_vmem, down_vmem,
            dma, dma((SLOTS,)), dma, dma,
            dma((BATCHES,)), dma((BATCHES,)), dma((BATCHES,)), dma((4,)), dma((2,)),
        ],
        compiler_params=pltpu.CompilerParams(
            collective_id=0, has_side_effects=True, vmem_limit_bytes=FORWARD_LIMIT
        ),
        cost_estimate=pl.CostEstimate(
            flops=2 * 10**10, bytes_accessed=4 * 10**7, transcendentals=0
        ),
        name="forward",
    )(cell_of, labels, features.reshape(CELLS_DEV, CELL, C), norm_gains, w_up, w_down)

    send = pl.pallas_call(
        layer_kernel,
        out_shape=slab,
        in_specs=[smem_spec(), smem_spec()] + [vmem_spec()] * 5,
        out_specs=vmem_spec(),
        scratch_shapes=[
            pltpu.VMEM((2, PATCH_ROWS + 2 * TK, C), jnp.float32),
            pltpu.VMEM((GROUPS, PATCH_ROWS, GROUP_LANES), jnp.bfloat16),
            pltpu.VMEM((GROUPS, PATCH_ROWS, GROUP_LANES), jnp.bfloat16),
            pltpu.VMEM((GROUPS, GROUP_LANES + DEPTH, PATCH_ROWS), jnp.bfloat16),
            pltpu.VMEM((HALF_ROWS, C), jnp.bfloat16),
            pltpu.VMEM((2, PATCH_ROWS, STACK), jnp.float32),
            pltpu.VMEM((2, PATCH_ROWS, STACK), jnp.float32),
            pltpu.SMEM((CELLS_DEV,), jnp.int32),
            pltpu.SMEM((SLOTS + 1,), jnp.int32),
            pltpu.SMEM((SLOTS + 1,), jnp.int32),
        ],
        compiler_params=pltpu.CompilerParams(vmem_limit_bytes=LAYER_LIMIT),
        cost_estimate=pl.CostEstimate(
            flops=2 * 10**10, bytes_accessed=4 * 10**7, transcendentals=0
        ),
        name="layer",
    )(
        own_labels.reshape(SLOTS, 128), other_labels.reshape(SLOTS, 128), own, other, norm_gains,
        w_qkv, w_out,
    )

    out = pl.pallas_call(
        return_kernel,
        out_shape=jax.ShapeDtypeStruct((CELLS_DEV, CELL, C), jnp.bfloat16),
        in_specs=[smem_spec(), smem_spec(), any_spec(), vmem_spec(), hbm_spec(), hbm_spec()],
        out_specs=vmem_spec(),
        scratch_shapes=[
            slab_vmem, slab_vmem, up_vmem, down_vmem, dma, dma((SLOTS,)), dma((2,)),
        ],
        compiler_params=pltpu.CompilerParams(
            collective_id=1, has_side_effects=True, vmem_limit_bytes=RETURN_LIMIT
        ),
        cost_estimate=pl.CostEstimate(
            flops=2 * 10**10, bytes_accessed=4 * 10**7, transcendentals=0
        ),
        name="homeward",
    )(slots, valid_count, send, norm_gains, w_up, w_down)
    return out.reshape(features.shape)


def solution(mesh):
    in_specs = (
        P("cells", "patch", None),
        P("cells", "patch"),
        P("cells", "patch"),
        P(),
        P(),
        P(),
        P(),
        P(),
    )
    out_specs = P("cells", "patch", None)
    return jax.shard_map(shards, mesh=mesh, in_specs=in_specs, out_specs=out_specs, check_vma=False)
```
